32 devices in a mesh: sect: 2 (over x), seq: 4 (over y, core), dp: 4 (over z).
Axes of the slice: x: 2, y: 2, z: 4, core: 2. Of those that a mesh axis runs over, the one named last changes fastest.
Arguments:
- query_tiles: bfloat16 [4, 8, 128, 2048], P('dp', None, 'sect', 'seq'), may hold values from -6 to 6
- key_tiles: bfloat16 [4, 8, 128, 2048], P('dp', None, 'sect', 'seq'), may hold values from -6 to 6
- value_tiles: bfloat16 [4, 8, 128, 2048], P('dp', None, 'sect', 'seq'), may hold values from -6 to 6
- text_keys: bfloat16 [8, 256, 2048], P(('sect', 'dp'), 'seq'), may hold values from -6 to 6
- text_values: bfloat16 [8, 256, 2048], P(('sect', 'dp'), 'seq'), may hold values from -6 to 6
- text_lengths: int32 [8], P(('sect', 'dp')), may hold values from 32 to 256, as said below
- tile_place: int32 [4], replicated, may hold values from 0 to 3, each once
Outputs:
- attended: bfloat16 [8, 512, 2048], P(('sect', 'dp'), 'seq')
The draws below stay inside these ranges and needn't reach their ends.
Inputs may be any that keep to these rules, and one draw needn't show every extreme that they name: `tile_place`: each spatial position is held by exactly one tile slot. `text_lengths`: the live text tokens of a clip are its first rows; some clip fills all 256 slots.
All inputs are finite; a program needn't handle non-finite values.
Results may differ from the reference program's by a relative error of at most 0.0031.
Values may be sent and summed in bfloat16 or wider, within the bound.
A program may use at most 64 MiB of HBM per device.

```python
import math
import jax
import jax.numpy as jnp
from jax import lax

HD = 128
HEADS = 16
TEXT = 256
TILES = 4
BLOCKS = 4
CLIPS = 8
TILE_ROWS = 32
TILE_SEQ = 128
TOKENS = 512
QW = 2048


def joint_draw(key):
    base = jax.random.fold_in(key, 11)
    key_query, key_keys = jax.random.split(base, 2)
    full_shape = (TILES, CLIPS, TILE_SEQ, HEADS * HD)
    queries = 1.6 * jax.random.truncated_normal(key_query, -3.75, 3.75, full_shape, jnp.float32)
    keys_all = 1.6 * jax.random.truncated_normal(key_keys, -3.75, 3.75, full_shape, jnp.float32)
    return (queries, keys_all)


def draw_query_tiles(key, part):
    return joint_draw(key)[0].astype(jnp.bfloat16)


def draw_key_tiles(key, part):
    return joint_draw(key)[1].astype(jnp.bfloat16)


def draw_text_lengths(key, part):
    base = jax.random.fold_in(key, 23)
    first_key, second_key = jax.random.split(base, 2)
    lengths = jax.random.randint(first_key, (CLIPS,), TEXT // 8, TEXT + 1).astype(jnp.int32)
    filled = jax.random.randint(second_key, (), 0, CLIPS)
    return lengths.at[filled].set(TEXT).astype(jnp.int32)


def steps_of(stream_key, dims, shards, low, largest):
    level = 1.0
    for position, shards_of in shards:
        draws = jax.random.uniform(jax.random.fold_in(jax.random.fold_in(stream_key, 6), position), (shards_of,), jnp.float32, low / len(shards), largest / len(shards))
        level = level * jnp.repeat(jnp.exp(draws), dims[position] // shards_of).reshape((-1,) + (1,) * (len(dims) - 1 - position))
    return level


def scatter_about(key, shape, deviation, reach, cuts=(), kind=jnp.bfloat16):
    drawn = deviation * jax.random.normal(key, shape, jnp.float32)
    if cuts:
        drawn = drawn * steps_of(key, shape, cuts, -0.22, 0.18)
    return jnp.clip(drawn, -reach, reach).astype(kind)


def setup_inputs(seed: int = 0) -> dict:
    key_of = jax.random.split(jax.random.key(seed), 8)
    return {
        "query_tiles": draw_query_tiles(jax.random.fold_in(key_of[7], 71), 0),
        "key_tiles": draw_key_tiles(jax.random.fold_in(key_of[7], 71), 0),
        "value_tiles": scatter_about(key_of[2], (TILES, CLIPS, TILE_SEQ, QW), 1.0, 6.0, ((0, 4), (2, 2), (3, 4))),
        "text_keys": scatter_about(key_of[3], (CLIPS, TEXT, QW), 1.6, 6.0, ((0, 8), (1, 4))),
        "text_values": scatter_about(key_of[4], (CLIPS, TEXT, QW), 1.0, 6.0, ((0, 8), (1, 4))),
        "text_lengths": draw_text_lengths(jax.random.fold_in(key_of[7], 71), 0),
        "tile_place": jax.random.permutation(key_of[6], TILES).astype(jnp.int32),
    }


def reference(query_tiles, key_tiles, value_tiles, text_keys, text_values, text_lengths, tile_place):
    inverse = jnp.argsort(tile_place).astype(jnp.int32)

    def assemble(tiles):
        placed = jnp.take(tiles, inverse, axis=0)
        placed = placed.reshape(TILES, CLIPS, BLOCKS, TILE_ROWS, HEADS, HD)
        placed = jnp.transpose(placed, (1, 2, 0, 3, 4, 5))
        return placed.reshape(CLIPS, TOKENS, HEADS, HD)
    video_queries = assemble(query_tiles)
    video_keys = assemble(key_tiles)
    video_values = assemble(value_tiles)
    text_key_rows = text_keys.reshape(CLIPS, TEXT, HEADS, HD)
    text_value_rows = text_values.reshape(CLIPS, TEXT, HEADS, HD)
    score_scale = 1.0 / math.sqrt(HD)

    def one_clip(operands):
        queries, keys_video, values_video, keys_text, values_text, length = operands
        all_keys = jnp.concatenate([keys_video, keys_text], 0).astype(jnp.float32)
        all_values = jnp.concatenate([values_video, values_text], 0).astype(jnp.float32)
        live_mask = jnp.concatenate([jnp.ones((TOKENS,), bool), jnp.arange(TEXT, dtype=jnp.int32) < length])
        scores = jnp.einsum('qhd,khd->hqk', queries.astype(jnp.float32), all_keys) * score_scale
        scores = jnp.where(live_mask[None, None, :], scores, -jnp.inf)
        row_max = lax.optimization_barrier(jnp.max(scores, axis=-1, keepdims=True))
        exponentials = jnp.exp(scores - row_max)
        denominators = lax.optimization_barrier(jnp.sum(exponentials, axis=-1))
        weights = lax.optimization_barrier(exponentials.astype(jnp.bfloat16))
        mixed = jnp.einsum('hqk,khd->qhd', weights.astype(jnp.float32), all_values)
        return (mixed / jnp.transpose(denominators)[:, :, None]).astype(jnp.bfloat16)
    attended = lax.map(one_clip, (video_queries, video_keys, video_values, text_key_rows, text_value_rows, text_lengths))
    return attended.reshape(CLIPS, TOKENS, HEADS * HD)
```

```python
import functools
import math

import jax
import jax.numpy as jnp
from jax import lax
from jax.experimental import pallas as pl
from jax.experimental.pallas import tpu as pltpu
from jax.sharding import PartitionSpec as P

HD = 128


def attend(queries_flat, keys_video, values_video, keys_text, values_text, length):
    query_rows, head_width = queries_flat.shape
    head_count = head_width // HD
    score_scale = 1.0 / math.sqrt(HD)
    keys_video = keys_video.reshape(-1, head_count, HD)
    values_video = values_video.reshape(-1, head_count, HD)
    keys_text = keys_text.reshape(-1, head_count, HD)
    values_text = values_text.reshape(-1, head_count, HD)
    live_mask = jnp.arange(keys_text.shape[0], dtype=jnp.int32) < length
    block_rows = math.gcd(query_rows, 512)

    def one_block(query_block):
        score_video = (
            jnp.einsum("qhd,khd->hqk", query_block, keys_video, preferred_element_type=jnp.float32)
            * score_scale
        )
        score_text = (
            jnp.einsum("qhd,khd->hqk", query_block, keys_text, preferred_element_type=jnp.float32)
            * score_scale
        )
        score_text = jnp.where(live_mask[None, None, :], score_text, -jnp.inf)
        row_max = jnp.maximum(jnp.max(score_video, axis=-1), jnp.max(score_text, axis=-1))[
            ..., None
        ]
        expo_video = jnp.exp(score_video - row_max)
        expo_text = jnp.exp(score_text - row_max)
        denominators = jnp.sum(expo_video, axis=-1) + jnp.sum(expo_text, axis=-1)
        mixed = jnp.einsum(
            "hqk,khd->qhd",
            expo_video.astype(jnp.bfloat16),
            values_video,
            preferred_element_type=jnp.float32,
        )
        mixed = mixed + jnp.einsum(
            "hqk,khd->qhd",
            expo_text.astype(jnp.bfloat16),
            values_text,
            preferred_element_type=jnp.float32,
        )
        return (mixed / jnp.transpose(denominators)[:, :, None]).astype(jnp.bfloat16)

    blocks = queries_flat.reshape(query_rows // block_rows, block_rows, head_count, HD)
    return lax.map(one_block, blocks).reshape(query_rows, head_width)


def shards(query_tiles, key_tiles, value_tiles, text_keys, text_values, text_lengths, tile_place):
    tile_count = lax.axis_size("dp")
    sect_count = lax.axis_size("sect")
    part_rows = query_tiles.shape[2]
    head_width = query_tiles.shape[3]
    tile_seq = part_rows * sect_count

    def regroup(piece):
        return piece.reshape(1, sect_count, tile_count, part_rows, head_width)

    relayed = (
        lax.all_to_all(
            lax.all_to_all(regroup(query_tiles), "sect", split_axis=1, concat_axis=3, tiled=True),
            "dp",
            split_axis=2,
            concat_axis=0,
            tiled=True,
        ),
        lax.all_to_all(
            lax.all_to_all(regroup(key_tiles), "sect", split_axis=1, concat_axis=3, tiled=True),
            "dp",
            split_axis=2,
            concat_axis=0,
            tiled=True,
        ),
        lax.all_to_all(
            lax.all_to_all(regroup(value_tiles), "sect", split_axis=1, concat_axis=3, tiled=True),
            "dp",
            split_axis=2,
            concat_axis=0,
            tiled=True,
        ),
    )
    spatial_order = jnp.argsort(tile_place)
    seq_count = lax.axis_size("seq")
    tile_rows = tile_seq // seq_count

    def arrange(piece):
        grid = piece.reshape(tile_count, seq_count, tile_rows, head_width)
        placed = jnp.concatenate(
            [lax.dynamic_slice_in_dim(grid, spatial_order[place], 1, axis=0) for place in range(tile_count)],
            axis=0,
        )
        placed = jnp.transpose(placed, (1, 0, 2, 3))
        return placed.reshape(seq_count * tile_count * tile_rows, head_width)

    video_queries = arrange(relayed[0])
    video_keys = arrange(relayed[1])
    video_values = arrange(relayed[2])
    keys_text, values_text = (
        lax.all_to_all(text_keys[0], "seq", split_axis=1, concat_axis=0, tiled=True),
        lax.all_to_all(text_values[0], "seq", split_axis=1, concat_axis=0, tiled=True),
    )
    attended_heads = attend(
        video_queries, video_keys, video_values, keys_text, values_text, text_lengths[0]
    )
    attended = lax.all_to_all(attended_heads, "seq", split_axis=0, concat_axis=1, tiled=True)
    return attended[None]


def peer_order(sect_count, tile_count):
    half = tile_count // 2
    steps = sorted(range(tile_count), key=lambda step: abs(step - half))
    pairs = [(o, step) for step in steps for o in reversed(range(sect_count))]
    pairs = [pair for pair in pairs if pair != (0, 0)]
    return pairs


def relay_kernel(
    sizes,
    chunks,
    q_ref, k_ref, v_ref, tk_ref, tv_ref, len_in, place_in,
    out_ref,
    qbuf, kbuf, vbuf, tbuf, obuf, len_ref, place_ref,
    send_sem, recv_sem, text_send, text_recv, out_send, out_recv, scalar_sems,
):
    sect_count, seq_count, tile_count, heads, part_blocks, rows, text_part = sizes
    me_s, me_q, me_d = lax.axis_index("sect"), lax.axis_index("seq"), lax.axis_index("dp")
    mesh_ids = pl.DeviceIdType.MESH
    width = heads * HD
    order = peer_order(sect_count, tile_count)
    block_rows = tile_count * rows
    text_rows = text_part * seq_count
    key_rows = block_rows * seq_count

    def group_peer(offset):
        return lax.rem(me_s + offset[0], sect_count), lax.rem(me_d + offset[1], tile_count)

    barrier = pltpu.get_barrier_semaphore()
    for offset in order:
        to_s, to_d = group_peer(offset)
        pl.semaphore_signal(barrier, inc=1, device_id={"sect": to_s, "dp": to_d}, device_id_type=mesh_ids)
    for step in range(1, seq_count):
        to_q = lax.rem(me_q + step, seq_count)
        pl.semaphore_signal(barrier, inc=1, device_id={"seq": to_q}, device_id_type=mesh_ids)
    scalars = (
        pltpu.make_async_copy(len_in, len_ref, scalar_sems.at[0]),
        pltpu.make_async_copy(place_in, place_ref, scalar_sems.at[1]),
    )
    for copy in scalars:
        copy.start()

    sources = (q_ref, k_ref, v_ref)
    buffers = (qbuf, kbuf, vbuf)
    texts = (tk_ref, tv_ref)

    def columns_of(chunk):
        return pl.ds(chunk[1] * HD, chunk[2] * HD)

    def pieces(chunk, clip):
        number, cut = chunk[0], chunk[3]
        for at in range(part_blocks if cut else 1):
            some = pl.ds(at, 1) if cut else pl.ds(0, part_blocks)
            there = pl.ds(me_s * part_blocks + at, 1) if cut else pl.ds(me_s * part_blocks, part_blocks)
            arrival = recv_sem.at[chunks.index(chunk), me_s * part_blocks + at if cut else 0]
            yield (
                sources[number].at[clip, some, :, columns_of(chunk)],
                buffers[number].at[there, me_d, :, columns_of(chunk)],
                arrival,
            )

    def send_chunk(chunk):
        for offset in order:
            to_s, to_d = group_peer(offset)
            for source, target, arrival in pieces(chunk, to_s * tile_count + to_d):
                pltpu.make_async_remote_copy(
                    src_ref=source,
                    dst_ref=target,
                    send_sem=send_sem.at[chunk[0]],
                    recv_sem=arrival,
                    device_id={"sect": to_s, "dp": to_d},
                    device_id_type=mesh_ids,
                ).start()

    for chunk in chunks:
        for source, target, arrival in pieces(chunk, me_s * tile_count + me_d):
            pltpu.make_async_copy(source, target, arrival).start()
    my_text = pl.ds(me_q * text_part, text_part)
    for number in range(2):
        pltpu.make_async_copy(
            texts[number].at[:, pl.ds(pl.multiple_of(me_q * width, HD), width)],
            tbuf.at[number, my_text],
            text_recv,
        ).start()

    pl.semaphore_wait(barrier, len(order) + seq_count - 1)

    send_chunk(chunks[0])
    for step in range(1, seq_count):
        to_q = lax.rem(me_q + step, seq_count)
        for number in range(2):
            pltpu.make_async_remote_copy(
                src_ref=texts[number].at[:, pl.ds(pl.multiple_of(to_q * width, HD), width)],
                dst_ref=tbuf.at[number, my_text],
                send_sem=text_send,
                recv_sem=text_recv,
                device_id={"seq": to_q},
                device_id_type=mesh_ids,
            ).start()
    for chunk in chunks[1:]:
        send_chunk(chunk)

    factor = math.log2(math.e) / math.sqrt(HD)
    for copy in scalars:
        copy.wait()
    live = lax.broadcasted_iota(jnp.int32, (1, text_rows), 1) < len_ref[0]
    places = [place_ref[slot] for slot in range(tile_count)]
    pltpu.make_async_copy(tbuf, tbuf, text_recv).wait()
    contract_last = (((1,), (1,)), ((), ()))
    waited = set()

    def await_part(number, head, block):
        for index, chunk in enumerate(chunks):
            if chunk[0] != number or not chunk[1] <= head < chunk[1] + chunk[2]:
                continue
            if chunk[3]:
                view = buffers[number].at[block, :, :, columns_of(chunk)]
                pltpu.make_async_copy(view, view, recv_sem.at[index, block]).wait()
            elif index not in waited:
                waited.add(index)
                view = buffers[number].at[:, :, :, columns_of(chunk)]
                pltpu.make_async_copy(view, view, recv_sem.at[index, 0]).wait()

    def in_place(tiles):
        placed = []
        for place in range(tile_count):
            chosen = tiles[0]
            for slot in range(1, tile_count):
                chosen = jnp.where(places[slot] == place, tiles[slot], chosen)
            placed.append(chosen)
        return jnp.concatenate(placed, axis=0)

    for c in range(heads):
        columns = slice(c * HD, (c + 1) * HD)
        await_part(1, c, None)
        keys = kbuf[:, :, :, columns].reshape(key_rows, HD)
        keys_text = tbuf[0, :, columns]
        await_part(2, c, None)
        values = vbuf[:, :, :, columns].reshape(key_rows, HD)
        values_text = tbuf[1, :, columns]
        for step in range(seq_count):
            flip = (2, 3, 1, 0)[step]
            to_q = jnp.bitwise_xor(me_q, flip)
            await_part(0, c, to_q)
            queries = in_place([qbuf[to_q, slot, :, columns] for slot in range(tile_count)])
            video = lax.dot_general(queries, keys, contract_last, preferred_element_type=jnp.float32)
            text = lax.dot_general(queries, keys_text, contract_last, preferred_element_type=jnp.float32)
            text = jnp.where(live, text, -jnp.inf)
            top = jnp.maximum(jnp.max(video, axis=1, keepdims=True), jnp.max(text, axis=1, keepdims=True))
            video = jnp.exp2((video - top) * factor)
            text = jnp.exp2((text - top) * factor)
            total = jnp.sum(video, axis=1, keepdims=True) + jnp.sum(text, axis=1, keepdims=True)
            mixed = jnp.dot(video.astype(jnp.bfloat16), values, preferred_element_type=jnp.float32)
            mixed += jnp.dot(text.astype(jnp.bfloat16), values_text, preferred_element_type=jnp.float32)
            obuf[c, step] = (mixed / total).astype(jnp.bfloat16)
            place = out_ref.at[:, pl.ds(pl.multiple_of((me_q * heads + c) * HD, HD), HD)]
            if flip == 0:
                pltpu.make_async_copy(obuf.at[c, step], place, out_recv).start()
            else:
                pltpu.make_async_remote_copy(
                    src_ref=obuf.at[c, step],
                    dst_ref=place,
                    send_sem=out_send,
                    recv_sem=out_recv,
                    device_id={"seq": to_q},
                    device_id_type=mesh_ids,
                ).start()

    for number in range(3):
        view = sources[number].at[pl.ds(0, len(order))]
        pltpu.make_async_copy(view, view, send_sem.at[number]).wait()
    text_view = tbuf.at[:, pl.ds(0, text_part * (seq_count - 1))]
    pltpu.make_async_copy(text_view, text_view, text_send).wait()
    out_view = obuf.at[:, pl.ds(0, seq_count - 1)]
    pltpu.make_async_copy(out_view, out_view, out_send).wait()
    pltpu.make_async_copy(out_ref, out_ref, out_recv).wait()


def relay_chunks(heads):
    chunks = [(number, 0, heads, False) for number in (1, 2)]
    chunks += [(0, c, 1, c == heads - 1) for c in range(heads)]
    return chunks


def fused_shards(query_tiles, key_tiles, value_tiles, text_keys, text_values, text_lengths, tile_place):
    sect_count, seq_count, tile_count = (lax.axis_size(name) for name in ("sect", "seq", "dp"))
    clips, part_rows, width = query_tiles.shape[1:]
    rows = part_rows * sect_count // seq_count
    heads = width // HD
    part_blocks = part_rows // rows
    text_part, all_width = text_keys.shape[1:]
    out_rows = tile_count * rows
    sizes = (sect_count, seq_count, tile_count, heads, part_blocks, rows, text_part)
    chunks = relay_chunks(heads)
    hbm = pl.BlockSpec(memory_space=pltpu.HBM)
    tiles = pltpu.VMEM((seq_count, tile_count, rows, width), jnp.bfloat16)

    def blocks(piece):
        return piece.reshape(clips, part_blocks, rows, width)

    gathered = pl.pallas_call(
        functools.partial(relay_kernel, sizes, chunks),
        out_shape=pltpu.VMEM((out_rows, all_width), jnp.bfloat16),
        in_specs=[hbm] * 7,
        out_specs=pl.BlockSpec(memory_space=pltpu.VMEM),
        scratch_shapes=[
            tiles,
            tiles,
            tiles,
            pltpu.VMEM((2, text_part * seq_count, width), jnp.bfloat16),
            pltpu.VMEM((heads, seq_count, out_rows, HD), jnp.bfloat16),
            pltpu.SMEM((1,), jnp.int32),
            pltpu.SMEM((tile_count,), jnp.int32),
            pltpu.SemaphoreType.DMA((3,)),
            pltpu.SemaphoreType.DMA((len(chunks), seq_count)),
            pltpu.SemaphoreType.DMA,
            pltpu.SemaphoreType.DMA,
            pltpu.SemaphoreType.DMA,
            pltpu.SemaphoreType.DMA,
            pltpu.SemaphoreType.DMA((2,)),
        ],
        compiler_params=pltpu.CompilerParams(
            collective_id=0, has_side_effects=True, vmem_limit_bytes=60 * 2**20
        ),
    )(
        blocks(query_tiles),
        blocks(key_tiles),
        blocks(value_tiles),
        text_keys[0],
        text_values[0],
        text_lengths,
        tile_place,
    )
    return gathered[None]


def solution(mesh):
    in_specs = (
        P("dp", None, "sect", "seq"),
        P("dp", None, "sect", "seq"),
        P("dp", None, "sect", "seq"),
        P(("sect", "dp"), "seq", None),
        P(("sect", "dp"), "seq", None),
        P(("sect", "dp")),
        P(),
    )
    out_specs = P(("sect", "dp"), "seq", None)

    def pick(*operands):
        rows = operands[0].shape[2] * mesh.shape["sect"] // mesh.shape["seq"]
        return (shards if rows % 16 or mesh.shape["seq"] != 4 else fused_shards)(*operands)

    return jax.shard_map(pick, mesh=mesh, in_specs=in_specs, out_specs=out_specs, check_vma=False)
```

```python
import functools
import math

import jax
import jax.numpy as jnp
from jax import lax
from jax.experimental import pallas as pl
from jax.experimental.pallas import tpu as pltpu
from jax.sharding import PartitionSpec as P

HD = 128


def attend(queries_flat, keys_video, values_video, keys_text, values_text, length):
    query_rows, head_width = queries_flat.shape
    head_count = head_width // HD
    score_scale = 1.0 / math.sqrt(HD)
    keys_video = keys_video.reshape(-1, head_count, HD)
    values_video = values_video.reshape(-1, head_count, HD)
    keys_text = keys_text.reshape(-1, head_count, HD)
    values_text = values_text.reshape(-1, head_count, HD)
    live_mask = jnp.arange(keys_text.shape[0], dtype=jnp.int32) < length
    block_rows = math.gcd(query_rows, 512)

    def one_block(query_block):
        score_video = (
            jnp.einsum("qhd,khd->hqk", query_block, keys_video, preferred_element_type=jnp.float32)
            * score_scale
        )
        score_text = (
            jnp.einsum("qhd,khd->hqk", query_block, keys_text, preferred_element_type=jnp.float32)
            * score_scale
        )
        score_text = jnp.where(live_mask[None, None, :], score_text, -jnp.inf)
        row_max = jnp.maximum(jnp.max(score_video, axis=-1), jnp.max(score_text, axis=-1))[
            ..., None
        ]
        expo_video = jnp.exp(score_video - row_max)
        expo_text = jnp.exp(score_text - row_max)
        denominators = jnp.sum(expo_video, axis=-1) + jnp.sum(expo_text, axis=-1)
        mixed = jnp.einsum(
            "hqk,khd->qhd",
            expo_video.astype(jnp.bfloat16),
            values_video,
            preferred_element_type=jnp.float32,
        )
        mixed = mixed + jnp.einsum(
            "hqk,khd->qhd",
            expo_text.astype(jnp.bfloat16),
            values_text,
            preferred_element_type=jnp.float32,
        )
        return (mixed / jnp.transpose(denominators)[:, :, None]).astype(jnp.bfloat16)

    blocks = queries_flat.reshape(query_rows // block_rows, block_rows, head_count, HD)
    return lax.map(one_block, blocks).reshape(query_rows, head_width)


def shards(query_tiles, key_tiles, value_tiles, text_keys, text_values, text_lengths, tile_place):
    tile_count = lax.axis_size("dp")
    sect_count = lax.axis_size("sect")
    part_rows = query_tiles.shape[2]
    head_width = query_tiles.shape[3]
    tile_seq = part_rows * sect_count

    def regroup(piece):
        return piece.reshape(1, sect_count, tile_count, part_rows, head_width)

    relayed = (
        lax.all_to_all(
            lax.all_to_all(regroup(query_tiles), "sect", split_axis=1, concat_axis=3, tiled=True),
            "dp",
            split_axis=2,
            concat_axis=0,
            tiled=True,
        ),
        lax.all_to_all(
            lax.all_to_all(regroup(key_tiles), "sect", split_axis=1, concat_axis=3, tiled=True),
            "dp",
            split_axis=2,
            concat_axis=0,
            tiled=True,
        ),
        lax.all_to_all(
            lax.all_to_all(regroup(value_tiles), "sect", split_axis=1, concat_axis=3, tiled=True),
            "dp",
            split_axis=2,
            concat_axis=0,
            tiled=True,
        ),
    )
    spatial_order = jnp.argsort(tile_place)
    seq_count = lax.axis_size("seq")
    tile_rows = tile_seq // seq_count

    def arrange(piece):
        grid = piece.reshape(tile_count, seq_count, tile_rows, head_width)
        placed = jnp.concatenate(
            [lax.dynamic_slice_in_dim(grid, spatial_order[place], 1, axis=0) for place in range(tile_count)],
            axis=0,
        )
        placed = jnp.transpose(placed, (1, 0, 2, 3))
        return placed.reshape(seq_count * tile_count * tile_rows, head_width)

    video_queries = arrange(relayed[0])
    video_keys = arrange(relayed[1])
    video_values = arrange(relayed[2])
    keys_text, values_text = (
        lax.all_to_all(text_keys[0], "seq", split_axis=1, concat_axis=0, tiled=True),
        lax.all_to_all(text_values[0], "seq", split_axis=1, concat_axis=0, tiled=True),
    )
    attended_heads = attend(
        video_queries, video_keys, video_values, keys_text, values_text, text_lengths[0]
    )
    attended = lax.all_to_all(attended_heads, "seq", split_axis=0, concat_axis=1, tiled=True)
    return attended[None]


def peer_order(sect_count, tile_count):
    half = tile_count // 2
    steps = sorted(range(tile_count), key=lambda step: abs(step - half))
    pairs = [(o, step) for step in steps for o in reversed(range(sect_count))]
    pairs = [pair for pair in pairs if pair != (0, 0)]
    return pairs


def relay_kernel(
    sizes,
    chunks,
    q_ref, k_ref, v_ref, tk_ref, tv_ref, len_in, place_in,
    out_ref,
    qbuf, kbuf, vbuf, tbuf, obuf, len_ref, place_ref,
    send_sem, recv_sem, text_send, text_recv, out_send, out_recv, scalar_sems, go_sem,
):
    sect_count, seq_count, tile_count, heads, part_blocks, rows, text_part = sizes
    me_s, me_q, me_d = lax.axis_index("sect"), lax.axis_index("seq"), lax.axis_index("dp")
    mesh_ids = pl.DeviceIdType.MESH
    width = heads * HD
    order = peer_order(sect_count, tile_count)
    block_rows = tile_count * rows
    text_rows = text_part * seq_count
    key_rows = block_rows * seq_count

    def group_peer(offset):
        return lax.rem(me_s + offset[0], sect_count), lax.rem(me_d + offset[1], tile_count)

    barrier = pltpu.get_barrier_semaphore()
    middle = jnp.logical_or(me_d == 1, me_d == 2)
    near = jnp.bitwise_xor(me_d, 3)
    side = jnp.bitwise_xor(me_d, 1)

    def greet(semaphore, flip, step, to_d):
        pl.semaphore_signal(
            semaphore,
            inc=1,
            device_id={
                "sect": jnp.bitwise_xor(me_s, flip),
                "seq": jnp.bitwise_xor(me_q, step),
                "dp": to_d,
            },
            device_id_type=mesh_ids,
        )

    @pl.when(middle)
    def _():
        greet(barrier, 0, 0, near)
        for step in range(seq_count):
            greet(barrier, 0, step, side)
        greet(barrier, 1, 0, side)
        for flip in range(sect_count):
            greet(barrier, flip, 0, jnp.bitwise_xor(me_d, 2))

    @pl.when(jnp.logical_not(middle))
    def _():
        greet(barrier, 1, 0, me_d)
        for flip in range(sect_count):
            greet(barrier, flip, 0, near)
        for step in range(1, seq_count):
            greet(barrier, 0, step, me_d)

    scalars = (
        pltpu.make_async_copy(len_in, len_ref, scalar_sems.at[0]),
        pltpu.make_async_copy(place_in, place_ref, scalar_sems.at[1]),
    )
    for copy in scalars:
        copy.start()

    sources = (q_ref, k_ref, v_ref)
    buffers = (qbuf, kbuf, vbuf)
    texts = (tk_ref, tv_ref)

    def columns_of(chunk):
        return pl.ds(chunk[1] * HD, chunk[2] * HD)

    def pieces(chunk, clip):
        number, cut = chunk[0], chunk[3]
        for at in range(part_blocks if cut else 1):
            some = pl.ds(at, 1) if cut else pl.ds(0, part_blocks)
            there = pl.ds(me_s * part_blocks + at, 1) if cut else pl.ds(me_s * part_blocks, part_blocks)
            arrival = recv_sem.at[chunks.index(chunk), me_s * part_blocks + at if cut else 0]
            yield (
                sources[number].at[clip, some, :, columns_of(chunk)],
                buffers[number].at[there, me_d, :, columns_of(chunk)],
                arrival,
            )

    def send_group(group, flip, turn):
        to_s = jnp.bitwise_xor(me_s, flip)
        to_d = jnp.bitwise_xor(me_d, turn)
        for chunk in group:
            for source, target, arrival in pieces(chunk, to_s * tile_count + to_d):
                pltpu.make_async_remote_copy(
                    src_ref=source,
                    dst_ref=target,
                    send_sem=send_sem.at[chunk[0]],
                    recv_sem=arrival,
                    device_id={"sect": to_s, "dp": to_d},
                    device_id_type=mesh_ids,
                ).start()

    my_text = pl.ds(me_q * text_part, text_part)

    def copy_own():
        for chunk in chunks:
            for source, target, arrival in pieces(chunk, me_s * tile_count + me_d):
                pltpu.make_async_copy(source, target, arrival).start()
        for number in range(2):
            pltpu.make_async_copy(
                texts[number].at[:, pl.ds(pl.multiple_of(me_q * width, HD), width)],
                tbuf.at[number, my_text],
                text_recv,
            ).start()

    def send_text():
        for step in range(1, seq_count):
            to_q = jnp.bitwise_xor(me_q, step)
            for number in range(2):
                pltpu.make_async_remote_copy(
                    src_ref=texts[number].at[:, pl.ds(pl.multiple_of(to_q * width, HD), width)],
                    dst_ref=tbuf.at[number, my_text],
                    send_sem=text_send,
                    recv_sem=text_recv,
                    device_id={"seq": to_q},
                    device_id_type=mesh_ids,
                ).start()

    def send_all(items):
        for item in items:
            if item == "text":
                send_text()
            elif item == "own":
                copy_own()
            elif item == "go":
                pl.semaphore_wait(go_sem, seq_count)
            else:
                for flip, turn in item[1]:
                    send_group(item[0], flip, turn)

    pl.semaphore_wait(barrier, jnp.where(middle, 1, 1 + sect_count + (seq_count - 1) * 2 + 1 + 1 + sect_count))

    @pl.when(jnp.logical_not(middle))
    def _():
        for step in range(seq_count):
            greet(go_sem, 0, step, side)


    pl.when(middle)(functools.partial(send_all, MIDS))
    pl.when(jnp.logical_not(middle))(functools.partial(send_all, ENDS))

    factor = math.log2(math.e) / math.sqrt(HD)
    for copy in scalars:
        copy.wait()
    live = lax.broadcasted_iota(jnp.int32, (1, text_rows), 1) < len_ref[0]
    places = [place_ref[slot] for slot in range(tile_count)]
    pltpu.make_async_copy(tbuf, tbuf, text_recv).wait()
    contract_last = (((1,), (1,)), ((), ()))
    waited = set()

    def await_part(number, head, block):
        for index, chunk in enumerate(chunks):
            if chunk[0] != number or not chunk[1] <= head < chunk[1] + chunk[2]:
                continue
            if chunk[3]:
                view = buffers[number].at[block, :, :, columns_of(chunk)]
                pltpu.make_async_copy(view, view, recv_sem.at[index, block]).wait()
            elif index not in waited:
                waited.add(index)
                view = buffers[number].at[:, :, :, columns_of(chunk)]
                pltpu.make_async_copy(view, view, recv_sem.at[index, 0]).wait()

    def in_place(tiles):
        placed = []
        for place in range(tile_count):
            chosen = tiles[0]
            for slot in range(1, tile_count):
                chosen = jnp.where(places[slot] == place, tiles[slot], chosen)
            placed.append(chosen)
        return jnp.concatenate(placed, axis=0)

    def attend_rows(queries, keys, values, keys_text, values_text):
        video = lax.dot_general(queries, keys, contract_last, preferred_element_type=jnp.float32)
        text = lax.dot_general(queries, keys_text, contract_last, preferred_element_type=jnp.float32)
        text = jnp.where(live, text, -jnp.inf)
        top = jnp.maximum(jnp.max(video, axis=1, keepdims=True), jnp.max(text, axis=1, keepdims=True))
        video = jnp.exp2((video - top) * factor)
        text = jnp.exp2((text - top) * factor)
        total = jnp.sum(video, axis=1, keepdims=True) + jnp.sum(text, axis=1, keepdims=True)
        mixed = jnp.dot(video.astype(jnp.bfloat16), values, preferred_element_type=jnp.float32)
        mixed += jnp.dot(text.astype(jnp.bfloat16), values_text, preferred_element_type=jnp.float32)
        return (mixed / total).astype(jnp.bfloat16)

    for c in range(heads):
        columns = slice(c * HD, (c + 1) * HD)
        await_part(1, c, None)
        await_part(2, c, None)
        keys = kbuf[:, :, :, columns].reshape(key_rows, HD)
        keys_text = tbuf[0, :, columns]
        values = vbuf[:, :, :, columns].reshape(key_rows, HD)
        values_text = tbuf[1, :, columns]
        place = out_ref.at[:, pl.ds(pl.multiple_of((me_q * heads + c) * HD, HD), HD)]
        for flips in PARTS[c]:
            owners = [jnp.bitwise_xor(me_q, flip) for flip in flips]
            for to_q in owners:
                await_part(0, c, to_q)
            queries = jnp.concatenate(
                [in_place([qbuf[to_q, slot, :, columns] for slot in range(tile_count)]) for to_q in owners],
                axis=0,
            )
            mixed = attend_rows(queries, keys, values, keys_text, values_text)
            for at, (flip, to_q) in enumerate(zip(flips, owners)):
                step = (2, 3, 1, 0).index(flip)
                obuf[c, step] = mixed[at * block_rows : (at + 1) * block_rows]
                if flip == 0:
                    pltpu.make_async_copy(obuf.at[c, step], place, out_recv).start()
                else:
                    pltpu.make_async_remote_copy(
                        src_ref=obuf.at[c, step],
                        dst_ref=place,
                        send_sem=out_send,
                        recv_sem=out_recv,
                        device_id={"seq": to_q},
                        device_id_type=mesh_ids,
                    ).start()

    for number in range(3):
        view = sources[number].at[pl.ds(0, len(order))]
        pltpu.make_async_copy(view, view, send_sem.at[number]).wait()
    text_view = tbuf.at[:, pl.ds(0, text_part * (seq_count - 1))]
    pltpu.make_async_copy(text_view, text_view, text_send).wait()
    out_view = obuf.at[:, pl.ds(0, seq_count - 1)]
    pltpu.make_async_copy(out_view, out_view, out_send).wait()
    pltpu.make_async_copy(out_ref, out_ref, out_recv).wait()


PARTS = [[(2, 3, 1, 0)], [(2, 3, 1, 0)], [(2, 3, 1, 0)], [(2, 3), (1, 0)]]
CHUNKS = [(1, 0, 2, False), (2, 0, 2, False), (0, 0, 2, False), (1, 2, 1, False), (2, 2, 1, False), (0, 2, 1, False), (1, 3, 1, False), (2, 3, 1, False), (0, 3, 1, False)]
ENDS = [([(1, 0, 2, False), (2, 0, 2, False), (0, 0, 2, False)], [(1, 3), (0, 3), (1, 2), (0, 2), (1, 1), (0, 1), (1, 0)]), 'own', 'text', ([(1, 2, 1, False), (2, 2, 1, False), (0, 2, 1, False)], [(1, 3), (0, 3), (1, 2), (0, 2), (1, 1), (0, 1), (1, 0)]), ([(1, 3, 1, False), (2, 3, 1, False)], [(1, 3), (0, 3), (1, 2), (0, 2), (1, 1), (0, 1), (1, 0)]), ([(0, 3, 1, False)], [(1, 3), (0, 3), (1, 2), (0, 2), (1, 1), (0, 1), (1, 0)])]
MIDS = [([(1, 0, 2, False), (2, 0, 2, False), (0, 0, 2, False)], [(0, 3)]), ([(1, 2, 1, False), (2, 2, 1, False), (0, 2, 1, False)], [(0, 3)]), 'own', 'go', 'text', ([(1, 0, 2, False), (2, 0, 2, False), (0, 0, 2, False)], [(1, 2), (0, 2), (1, 3)]), ([(1, 0, 2, False), (2, 0, 2, False), (0, 0, 2, False), (1, 2, 1, False), (2, 2, 1, False), (0, 2, 1, False), (1, 3, 1, False), (2, 3, 1, False), (0, 3, 1, False)], [(1, 1), (0, 1), (1, 0)]), ([(1, 2, 1, False), (2, 2, 1, False), (0, 2, 1, False)], [(1, 2), (0, 2)]), ([(1, 3, 1, False), (2, 3, 1, False)], [(1, 2), (0, 2)]), ([(0, 3, 1, False)], [(1, 2), (0, 2)]), ([(1, 2, 1, False), (2, 2, 1, False), (0, 2, 1, False)], [(1, 3)]), ([(1, 3, 1, False), (2, 3, 1, False)], [(1, 3), (0, 3)]), ([(0, 3, 1, False)], [(1, 3), (0, 3)])]


def relay_chunks(heads):
    return CHUNKS


def fused_shards(query_tiles, key_tiles, value_tiles, text_keys, text_values, text_lengths, tile_place):
    sect_count, seq_count, tile_count = (lax.axis_size(name) for name in ("sect", "seq", "dp"))
    clips, part_rows, width = query_tiles.shape[1:]
    rows = part_rows * sect_count // seq_count
    heads = width // HD
    part_blocks = part_rows // rows
    text_part, all_width = text_keys.shape[1:]
    out_rows = tile_count * rows
    sizes = (sect_count, seq_count, tile_count, heads, part_blocks, rows, text_part)
    chunks = relay_chunks(heads)
    hbm = pl.BlockSpec(memory_space=pltpu.HBM)
    tiles = pltpu.VMEM((seq_count, tile_count, rows, width), jnp.bfloat16)

    def blocks(piece):
        return piece.reshape(clips, part_blocks, rows, width)

    gathered = pl.pallas_call(
        functools.partial(relay_kernel, sizes, chunks),
        out_shape=pltpu.VMEM((out_rows, all_width), jnp.bfloat16),
        in_specs=[hbm] * 7,
        out_specs=pl.BlockSpec(memory_space=pltpu.VMEM),
        scratch_shapes=[
            tiles,
            tiles,
            tiles,
            pltpu.VMEM((2, text_part * seq_count, width), jnp.bfloat16),
            pltpu.VMEM((heads, seq_count, out_rows, HD), jnp.bfloat16),
            pltpu.SMEM((1,), jnp.int32),
            pltpu.SMEM((tile_count,), jnp.int32),
            pltpu.SemaphoreType.DMA((3,)),
            pltpu.SemaphoreType.DMA((len(chunks), seq_count)),
            pltpu.SemaphoreType.DMA,
            pltpu.SemaphoreType.DMA,
            pltpu.SemaphoreType.DMA,
            pltpu.SemaphoreType.DMA,
            pltpu.SemaphoreType.DMA((2,)),
            pltpu.SemaphoreType.REGULAR,
        ],
        compiler_params=pltpu.CompilerParams(
            collective_id=0, has_side_effects=True, vmem_limit_bytes=60 * 2**20
        ),
    )(
        blocks(query_tiles),
        blocks(key_tiles),
        blocks(value_tiles),
        text_keys[0],
        text_values[0],
        text_lengths,
        tile_place,
    )
    return gathered[None]


def solution(mesh):
    in_specs = (
        P("dp", None, "sect", "seq"),
        P("dp", None, "sect", "seq"),
        P("dp", None, "sect", "seq"),
        P(("sect", "dp"), "seq", None),
        P(("sect", "dp"), "seq", None),
        P(("sect", "dp")),
        P(),
    )
    out_specs = P(("sect", "dp"), "seq", None)

    def pick(*operands):
        rows = operands[0].shape[2] * mesh.shape["sect"] // mesh.shape["seq"]
        return (shards if rows % 16 or mesh.shape["seq"] != 4 else fused_shards)(*operands)

    return jax.shard_map(pick, mesh=mesh, in_specs=in_specs, out_specs=out_specs, check_vma=False)
```

```python
import functools
import math

import jax
import jax.numpy as jnp
from jax import lax
from jax.experimental import pallas as pl
from jax.experimental.pallas import tpu as pltpu
from jax.sharding import PartitionSpec as P

HD = 128


def attend(queries_flat, keys_video, values_video, keys_text, values_text, length):
    query_rows, head_width = queries_flat.shape
    head_count = head_width // HD
    score_scale = 1.0 / math.sqrt(HD)
    keys_video = keys_video.reshape(-1, head_count, HD)
    values_video = values_video.reshape(-1, head_count, HD)
    keys_text = keys_text.reshape(-1, head_count, HD)
    values_text = values_text.reshape(-1, head_count, HD)
    live_mask = jnp.arange(keys_text.shape[0], dtype=jnp.int32) < length
    block_rows = math.gcd(query_rows, 512)

    def one_block(query_block):
        score_video = (
            jnp.einsum("qhd,khd->hqk", query_block, keys_video, preferred_element_type=jnp.float32)
            * score_scale
        )
        score_text = (
            jnp.einsum("qhd,khd->hqk", query_block, keys_text, preferred_element_type=jnp.float32)
            * score_scale
        )
        score_text = jnp.where(live_mask[None, None, :], score_text, -jnp.inf)
        row_max = jnp.maximum(jnp.max(score_video, axis=-1), jnp.max(score_text, axis=-1))[
            ..., None
        ]
        expo_video = jnp.exp(score_video - row_max)
        expo_text = jnp.exp(score_text - row_max)
        denominators = jnp.sum(expo_video, axis=-1) + jnp.sum(expo_text, axis=-1)
        mixed = jnp.einsum(
            "hqk,khd->qhd",
            expo_video.astype(jnp.bfloat16),
            values_video,
            preferred_element_type=jnp.float32,
        )
        mixed = mixed + jnp.einsum(
            "hqk,khd->qhd",
            expo_text.astype(jnp.bfloat16),
            values_text,
            preferred_element_type=jnp.float32,
        )
        return (mixed / jnp.transpose(denominators)[:, :, None]).astype(jnp.bfloat16)

    blocks = queries_flat.reshape(query_rows // block_rows, block_rows, head_count, HD)
    return lax.map(one_block, blocks).reshape(query_rows, head_width)


def shards(query_tiles, key_tiles, value_tiles, text_keys, text_values, text_lengths, tile_place):
    tile_count = lax.axis_size("dp")
    sect_count = lax.axis_size("sect")
    part_rows = query_tiles.shape[2]
    head_width = query_tiles.shape[3]
    tile_seq = part_rows * sect_count

    def regroup(piece):
        return piece.reshape(1, sect_count, tile_count, part_rows, head_width)

    relayed = (
        lax.all_to_all(
            lax.all_to_all(regroup(query_tiles), "sect", split_axis=1, concat_axis=3, tiled=True),
            "dp",
            split_axis=2,
            concat_axis=0,
            tiled=True,
        ),
        lax.all_to_all(
            lax.all_to_all(regroup(key_tiles), "sect", split_axis=1, concat_axis=3, tiled=True),
            "dp",
            split_axis=2,
            concat_axis=0,
            tiled=True,
        ),
        lax.all_to_all(
            lax.all_to_all(regroup(value_tiles), "sect", split_axis=1, concat_axis=3, tiled=True),
            "dp",
            split_axis=2,
            concat_axis=0,
            tiled=True,
        ),
    )
    spatial_order = jnp.argsort(tile_place)
    seq_count = lax.axis_size("seq")
    tile_rows = tile_seq // seq_count

    def arrange(piece):
        grid = piece.reshape(tile_count, seq_count, tile_rows, head_width)
        placed = jnp.concatenate(
            [lax.dynamic_slice_in_dim(grid, spatial_order[place], 1, axis=0) for place in range(tile_count)],
            axis=0,
        )
        placed = jnp.transpose(placed, (1, 0, 2, 3))
        return placed.reshape(seq_count * tile_count * tile_rows, head_width)

    video_queries = arrange(relayed[0])
    video_keys = arrange(relayed[1])
    video_values = arrange(relayed[2])
    keys_text, values_text = (
        lax.all_to_all(text_keys[0], "seq", split_axis=1, concat_axis=0, tiled=True),
        lax.all_to_all(text_values[0], "seq", split_axis=1, concat_axis=0, tiled=True),
    )
    attended_heads = attend(
        video_queries, video_keys, video_values, keys_text, values_text, text_lengths[0]
    )
    attended = lax.all_to_all(attended_heads, "seq", split_axis=0, concat_axis=1, tiled=True)
    return attended[None]


def peer_order(sect_count, tile_count):
    half = tile_count // 2
    steps = sorted(range(tile_count), key=lambda step: abs(step - half))
    pairs = [(o, step) for step in steps for o in reversed(range(sect_count))]
    pairs = [pair for pair in pairs if pair != (0, 0)]
    return pairs


def relay_kernel(
    sizes,
    chunks,
    q_ref, k_ref, v_ref, tk_ref, tv_ref, len_in, place_in,
    out_ref,
    qbuf, kbuf, vbuf, tbuf, obuf, len_ref, place_ref,
    send_sem, recv_sem, text_send, text_recv, out_send, out_recv, scalar_sems, go_sem, pbuf, dbuf,
):
    sect_count, seq_count, tile_count, heads, part_blocks, rows, text_part = sizes
    me_s, me_q, me_d = lax.axis_index("sect"), lax.axis_index("seq"), lax.axis_index("dp")
    mesh_ids = pl.DeviceIdType.MESH
    width = heads * HD
    order = peer_order(sect_count, tile_count)
    block_rows = tile_count * rows
    text_rows = text_part * seq_count
    key_rows = block_rows * seq_count

    def group_peer(offset):
        return lax.rem(me_s + offset[0], sect_count), lax.rem(me_d + offset[1], tile_count)

    barrier = pltpu.get_barrier_semaphore()
    middle = jnp.logical_or(me_d == 1, me_d == 2)
    near = jnp.bitwise_xor(me_d, 3)
    side = jnp.bitwise_xor(me_d, 1)

    def greet(semaphore, flip, step, to_d):
        pl.semaphore_signal(
            semaphore,
            inc=1,
            device_id={
                "sect": jnp.bitwise_xor(me_s, flip),
                "seq": jnp.bitwise_xor(me_q, step),
                "dp": to_d,
            },
            device_id_type=mesh_ids,
        )

    @pl.when(middle)
    def _():
        greet(barrier, 0, 0, near)
        for step in range(seq_count):
            greet(barrier, 0, step, side)
        greet(barrier, 1, 0, side)
        for flip in range(sect_count):
            greet(barrier, flip, 0, jnp.bitwise_xor(me_d, 2))

    @pl.when(jnp.logical_not(middle))
    def _():
        greet(barrier, 1, 0, me_d)
        for flip in range(sect_count):
            greet(barrier, flip, 0, near)
        for step in range(1, seq_count):
            greet(barrier, 0, step, me_d)

    scalars = (
        pltpu.make_async_copy(len_in, len_ref, scalar_sems.at[0]),
        pltpu.make_async_copy(place_in, place_ref, scalar_sems.at[1]),
    )
    for copy in scalars:
        copy.start()

    sources = (q_ref, k_ref, v_ref)
    buffers = (qbuf, kbuf, vbuf)
    texts = (tk_ref, tv_ref)

    def columns_of(chunk):
        return pl.ds(chunk[1] * HD, chunk[2] * HD)

    def pieces(chunk, clip):
        number, cut = chunk[0], chunk[3]
        for at in range(part_blocks if cut else 1):
            some = pl.ds(at, 1) if cut else pl.ds(0, part_blocks)
            there = pl.ds(me_s * part_blocks + at, 1) if cut else pl.ds(me_s * part_blocks, part_blocks)
            arrival = recv_sem.at[chunks.index(chunk), me_s * part_blocks + at if cut else 0]
            yield (
                sources[number].at[clip, some, :, columns_of(chunk)],
                buffers[number].at[there, me_d, :, columns_of(chunk)],
                arrival,
            )

    def send_group(group, flip, turn):
        to_s = jnp.bitwise_xor(me_s, flip)
        to_d = jnp.bitwise_xor(me_d, turn)
        for chunk in group:
            for source, target, arrival in pieces(chunk, to_s * tile_count + to_d):
                pltpu.make_async_remote_copy(
                    src_ref=source,
                    dst_ref=target,
                    send_sem=send_sem.at[chunk[0]],
                    recv_sem=arrival,
                    device_id={"sect": to_s, "dp": to_d},
                    device_id_type=mesh_ids,
                ).start()

    my_text = pl.ds(me_q * text_part, text_part)

    def copy_own():
        for chunk in chunks:
            for source, target, arrival in pieces(chunk, me_s * tile_count + me_d):
                pltpu.make_async_copy(source, target, arrival).start()
        for number in range(2):
            pltpu.make_async_copy(
                texts[number].at[:, pl.ds(pl.multiple_of(me_q * width, HD), width)],
                tbuf.at[number, my_text],
                text_recv,
            ).start()

    def send_text():
        for step in range(1, seq_count):
            to_q = jnp.bitwise_xor(me_q, step)
            for number in range(2):
                pltpu.make_async_remote_copy(
                    src_ref=texts[number].at[:, pl.ds(pl.multiple_of(to_q * width, HD), width)],
                    dst_ref=tbuf.at[number, my_text],
                    send_sem=text_send,
                    recv_sem=text_recv,
                    device_id={"seq": to_q},
                    device_id_type=mesh_ids,
                ).start()

    def send_all(items):
        for item in items:
            if item == "text":
                send_text()
            elif item == "own":
                copy_own()
            elif item == "go":
                pl.semaphore_wait(go_sem, seq_count)
            else:
                for flip, turn in item[1]:
                    send_group(item[0], flip, turn)

    pl.semaphore_wait(barrier, jnp.where(middle, 1, 1 + sect_count + (seq_count - 1) * 2 + 1 + 1 + sect_count))

    @pl.when(jnp.logical_not(middle))
    def _():
        for step in range(seq_count):
            greet(go_sem, 0, step, side)


    pl.when(me_d == 1)(functools.partial(send_all, MIDS[1]))
    pl.when(me_d == 2)(functools.partial(send_all, MIDS[2]))
    pl.when(jnp.logical_not(middle))(functools.partial(send_all, ENDS))

    factor = math.log2(math.e) / math.sqrt(HD)
    for copy in scalars:
        copy.wait()
    live = lax.broadcasted_iota(jnp.int32, (1, text_rows), 1) < len_ref[0]
    places = [place_ref[slot] for slot in range(tile_count)]
    pltpu.make_async_copy(tbuf, tbuf, text_recv).wait()
    contract_last = (((1,), (1,)), ((), ()))
    waited = set()

    def await_part(number, head, block):
        for index, chunk in enumerate(chunks):
            if chunk[0] != number or not chunk[1] <= head < chunk[1] + chunk[2]:
                continue
            if chunk[3]:
                view = buffers[number].at[block, :, :, columns_of(chunk)]
                pltpu.make_async_copy(view, view, recv_sem.at[index, block]).wait()
            elif index not in waited:
                waited.add(index)
                view = buffers[number].at[:, :, :, columns_of(chunk)]
                pltpu.make_async_copy(view, view, recv_sem.at[index, 0]).wait()

    def in_place(tiles):
        placed = []
        for place in range(tile_count):
            chosen = tiles[0]
            for slot in range(1, tile_count):
                chosen = jnp.where(places[slot] == place, tiles[slot], chosen)
            placed.append(chosen)
        return jnp.concatenate(placed, axis=0)

    def scores_of(queries, keys, keys_text):
        video = lax.dot_general(queries, keys, contract_last, preferred_element_type=jnp.float32)
        text = lax.dot_general(queries, keys_text, contract_last, preferred_element_type=jnp.float32)
        text = jnp.where(live, text, -jnp.inf)
        top = jnp.maximum(jnp.max(video, axis=1, keepdims=True), jnp.max(text, axis=1, keepdims=True))
        video = jnp.exp2((video - top) * factor)
        text = jnp.exp2((text - top) * factor)
        total = jnp.sum(video, axis=1, keepdims=True) + jnp.sum(text, axis=1, keepdims=True)
        return video.astype(jnp.bfloat16), text.astype(jnp.bfloat16), total

    def mix(video, text, total, values, values_text):
        mixed = jnp.dot(video, values, preferred_element_type=jnp.float32)
        mixed += jnp.dot(text, values_text, preferred_element_type=jnp.float32)
        return (mixed / total).astype(jnp.bfloat16)

    def deliver(c, step, block):
        flip = FLIPS[step]
        obuf[c, step] = block
        place = out_ref.at[:, pl.ds(pl.multiple_of((me_q * heads + c) * HD, HD), HD)]
        if flip == 0:
            pltpu.make_async_copy(obuf.at[c, step], place, out_recv).start()
        else:
            pltpu.make_async_remote_copy(
                src_ref=obuf.at[c, step],
                dst_ref=place,
                send_sem=out_send,
                recv_sem=out_recv,
                device_id={"seq": jnp.bitwise_xor(me_q, flip)},
                device_id_type=mesh_ids,
            ).start()

    owners = [jnp.bitwise_xor(me_q, flip) for flip in FLIPS]
    for c in range(heads):
        columns = slice(c * HD, (c + 1) * HD)
        await_part(1, c, None)
        await_part(0, c, None)
        queries = jnp.concatenate(
            [in_place([qbuf[to_q, slot, :, columns] for slot in range(tile_count)]) for to_q in owners],
            axis=0,
        )
        keys = kbuf[:, :, :, columns].reshape(key_rows, HD)
        video, text, total = scores_of(queries, keys, tbuf[0, :, columns])
        if c == heads - 1:
            pbuf[:, :key_rows] = video
            pbuf[:, key_rows:] = text
            dbuf[...] = jnp.broadcast_to(total, dbuf.shape)
        await_part(2, c, None)
        values = vbuf[:, :, :, columns].reshape(key_rows, HD)
        values_text = tbuf[1, :, columns]
        if c < heads - 1:
            mixed = mix(video, text, total, values, values_text)
            for step in range(seq_count):
                deliver(c, step, mixed[step * block_rows : (step + 1) * block_rows])
        else:
            for half in range(HALVES):
                size = key_rows // HALVES
                some = slice(half * size, (half + 1) * size)
                mixed = mix(pbuf[some, :key_rows], pbuf[some, key_rows:], dbuf[some], values, values_text)
                for at in range(size // block_rows):
                    deliver(c, half * (size // block_rows) + at, mixed[at * block_rows : (at + 1) * block_rows])

    for number in range(3):
        view = sources[number].at[pl.ds(0, len(order))]
        pltpu.make_async_copy(view, view, send_sem.at[number]).wait()
    text_view = tbuf.at[:, pl.ds(0, text_part * (seq_count - 1))]
    pltpu.make_async_copy(text_view, text_view, text_send).wait()
    out_view = obuf.at[:, pl.ds(0, seq_count - 1)]
    pltpu.make_async_copy(out_view, out_view, out_send).wait()
    pltpu.make_async_copy(out_ref, out_ref, out_recv).wait()


FLIPS = (2, 3, 1, 0)
HALVES = 2
CHUNKS = [(1, 0, 2, False), (2, 0, 2, False), (0, 0, 2, False), (1, 2, 1, False), (2, 2, 1, False), (0, 2, 1, False), (1, 3, 1, False), (0, 3, 1, False), (2, 3, 1, False)]
ENDS = [([(1, 0, 2, False), (2, 0, 2, False), (0, 0, 2, False)], [(1, 2), (0, 2), (1, 3), (0, 3), (1, 1), (0, 1), (1, 0)]), 'own', 'text', ([(1, 2, 1, False), (2, 2, 1, False), (0, 2, 1, False)], [(1, 2), (0, 2), (1, 3), (0, 3), (1, 1), (0, 1), (1, 0)]), ([(1, 3, 1, False), (0, 3, 1, False)], [(1, 2), (0, 2), (1, 3), (0, 3), (1, 1), (0, 1), (1, 0)]), ([(2, 3, 1, False)], [(1, 2), (0, 2), (1, 3), (0, 3), (1, 1), (0, 1), (1, 0)])]
MIDS = {2: [([(1, 0, 2, False), (2, 0, 2, False), (0, 0, 2, False)], [(0, 3)]), 'own', 'go', 'text', ([(1, 0, 2, False), (2, 0, 2, False), (0, 0, 2, False)], [(1, 2), (0, 2), (1, 3)]), ([(1, 0, 2, False), (2, 0, 2, False), (0, 0, 2, False), (1, 2, 1, False), (2, 2, 1, False), (0, 2, 1, False), (1, 3, 1, False), (0, 3, 1, False), (2, 3, 1, False)], [(1, 1), (0, 1), (1, 0)]), ([(1, 2, 1, False), (2, 2, 1, False), (0, 2, 1, False)], [(1, 2), (0, 2)]), ([(1, 3, 1, False), (0, 3, 1, False)], [(1, 2), (0, 2)]), ([(2, 3, 1, False)], [(1, 2), (0, 2)]), ([(1, 2, 1, False), (2, 2, 1, False), (0, 2, 1, False)], [(1, 3), (0, 3)]), ([(1, 3, 1, False), (0, 3, 1, False)], [(1, 3), (0, 3)]), ([(2, 3, 1, False)], [(1, 3), (0, 3)])],
    1: [([(1, 0, 2, False), (2, 0, 2, False), (0, 0, 2, False)], [(0, 3)]), 'own', 'go', 'text', ([(1, 0, 2, False), (2, 0, 2, False), (0, 0, 2, False)], [(1, 2), (0, 2), (1, 3)]), ([(1, 0, 2, False), (2, 0, 2, False), (0, 0, 2, False), (1, 2, 1, False), (2, 2, 1, False), (0, 2, 1, False), (1, 3, 1, False), (0, 3, 1, False), (2, 3, 1, False)], [(1, 1), (0, 1), (1, 0)]), ([(1, 2, 1, False), (2, 2, 1, False), (0, 2, 1, False)], [(1, 2), (0, 2)]), ([(1, 3, 1, False), (0, 3, 1, False)], [(1, 2), (0, 2)]), ([(1, 2, 1, False), (2, 2, 1, False), (0, 2, 1, False)], [(1, 3), (0, 3)]), ([(1, 3, 1, False), (0, 3, 1, False)], [(1, 3), (0, 3)]), ([(2, 3, 1, False)], [(1, 3), (0, 3)]), ([(2, 3, 1, False)], [(1, 2), (0, 2)])]}


def relay_chunks(heads):
    return CHUNKS


def fused_shards(query_tiles, key_tiles, value_tiles, text_keys, text_values, text_lengths, tile_place):
    sect_count, seq_count, tile_count = (lax.axis_size(name) for name in ("sect", "seq", "dp"))
    clips, part_rows, width = query_tiles.shape[1:]
    rows = part_rows * sect_count // seq_count
    heads = width // HD
    part_blocks = part_rows // rows
    text_part, all_width = text_keys.shape[1:]
    out_rows = tile_count * rows
    sizes = (sect_count, seq_count, tile_count, heads, part_blocks, rows, text_part)
    chunks = relay_chunks(heads)
    hbm = pl.BlockSpec(memory_space=pltpu.HBM)
    tiles = pltpu.VMEM((seq_count, tile_count, rows, width), jnp.bfloat16)

    def blocks(piece):
        return piece.reshape(clips, part_blocks, rows, width)

    gathered = pl.pallas_call(
        functools.partial(relay_kernel, sizes, chunks),
        out_shape=pltpu.VMEM((out_rows, all_width), jnp.bfloat16),
        in_specs=[hbm] * 7,
        out_specs=pl.BlockSpec(memory_space=pltpu.VMEM),
        scratch_shapes=[
            tiles,
            tiles,
            tiles,
            pltpu.VMEM((2, text_part * seq_count, width), jnp.bfloat16),
            pltpu.VMEM((heads, seq_count, out_rows, HD), jnp.bfloat16),
            pltpu.SMEM((1,), jnp.int32),
            pltpu.SMEM((tile_count,), jnp.int32),
            pltpu.SemaphoreType.DMA((3,)),
            pltpu.SemaphoreType.DMA((len(chunks), seq_count)),
            pltpu.SemaphoreType.DMA,
            pltpu.SemaphoreType.DMA,
            pltpu.SemaphoreType.DMA,
            pltpu.SemaphoreType.DMA,
            pltpu.SemaphoreType.DMA((2,)),
            pltpu.SemaphoreType.REGULAR,
            pltpu.VMEM((seq_count * out_rows, seq_count * (out_rows + text_part)), jnp.bfloat16),
            pltpu.VMEM((seq_count * out_rows, HD), jnp.float32),
        ],
        compiler_params=pltpu.CompilerParams(
            collective_id=0, has_side_effects=True, vmem_limit_bytes=60 * 2**20
        ),
    )(
        blocks(query_tiles),
        blocks(key_tiles),
        blocks(value_tiles),
        text_keys[0],
        text_values[0],
        text_lengths,
        tile_place,
    )
    return gathered[None]


def solution(mesh):
    in_specs = (
        P("dp", None, "sect", "seq"),
        P("dp", None, "sect", "seq"),
        P("dp", None, "sect", "seq"),
        P(("sect", "dp"), "seq", None),
        P(("sect", "dp"), "seq", None),
        P(("sect", "dp")),
        P(),
    )
    out_specs = P(("sect", "dp"), "seq", None)

    def pick(*operands):
        rows = operands[0].shape[2] * mesh.shape["sect"] // mesh.shape["seq"]
        return (shards if rows % 16 or mesh.shape["seq"] != 4 else fused_shards)(*operands)

    return jax.shard_map(pick, mesh=mesh, in_specs=in_specs, out_specs=out_specs, check_vma=False)
```

```python
import functools
import math

import jax
import jax.numpy as jnp
from jax import lax
from jax.experimental import pallas as pl
from jax.experimental.pallas import tpu as pltpu
from jax.sharding import PartitionSpec as P

HD = 128


def attend(queries_flat, keys_video, values_video, keys_text, values_text, length):
    query_rows, head_width = queries_flat.shape
    head_count = head_width // HD
    score_scale = 1.0 / math.sqrt(HD)
    keys_video = keys_video.reshape(-1, head_count, HD)
    values_video = values_video.reshape(-1, head_count, HD)
    keys_text = keys_text.reshape(-1, head_count, HD)
    values_text = values_text.reshape(-1, head_count, HD)
    live_mask = jnp.arange(keys_text.shape[0], dtype=jnp.int32) < length
    block_rows = math.gcd(query_rows, 512)

    def one_block(query_block):
        score_video = (
            jnp.einsum("qhd,khd->hqk", query_block, keys_video, preferred_element_type=jnp.float32)
            * score_scale
        )
        score_text = (
            jnp.einsum("qhd,khd->hqk", query_block, keys_text, preferred_element_type=jnp.float32)
            * score_scale
        )
        score_text = jnp.where(live_mask[None, None, :], score_text, -jnp.inf)
        row_max = jnp.maximum(jnp.max(score_video, axis=-1), jnp.max(score_text, axis=-1))[
            ..., None
        ]
        expo_video = jnp.exp(score_video - row_max)
        expo_text = jnp.exp(score_text - row_max)
        denominators = jnp.sum(expo_video, axis=-1) + jnp.sum(expo_text, axis=-1)
        mixed = jnp.einsum(
            "hqk,khd->qhd",
            expo_video.astype(jnp.bfloat16),
            values_video,
            preferred_element_type=jnp.float32,
        )
        mixed = mixed + jnp.einsum(
            "hqk,khd->qhd",
            expo_text.astype(jnp.bfloat16),
            values_text,
            preferred_element_type=jnp.float32,
        )
        return (mixed / jnp.transpose(denominators)[:, :, None]).astype(jnp.bfloat16)

    blocks = queries_flat.reshape(query_rows // block_rows, block_rows, head_count, HD)
    return lax.map(one_block, blocks).reshape(query_rows, head_width)


def shards(query_tiles, key_tiles, value_tiles, text_keys, text_values, text_lengths, tile_place):
    tile_count = lax.axis_size("dp")
    sect_count = lax.axis_size("sect")
    part_rows = query_tiles.shape[2]
    head_width = query_tiles.shape[3]
    tile_seq = part_rows * sect_count

    def regroup(piece):
        return piece.reshape(1, sect_count, tile_count, part_rows, head_width)

    relayed = (
        lax.all_to_all(
            lax.all_to_all(regroup(query_tiles), "sect", split_axis=1, concat_axis=3, tiled=True),
            "dp",
            split_axis=2,
            concat_axis=0,
            tiled=True,
        ),
        lax.all_to_all(
            lax.all_to_all(regroup(key_tiles), "sect", split_axis=1, concat_axis=3, tiled=True),
            "dp",
            split_axis=2,
            concat_axis=0,
            tiled=True,
        ),
        lax.all_to_all(
            lax.all_to_all(regroup(value_tiles), "sect", split_axis=1, concat_axis=3, tiled=True),
            "dp",
            split_axis=2,
            concat_axis=0,
            tiled=True,
        ),
    )
    spatial_order = jnp.argsort(tile_place)
    seq_count = lax.axis_size("seq")
    tile_rows = tile_seq // seq_count

    def arrange(piece):
        grid = piece.reshape(tile_count, seq_count, tile_rows, head_width)
        placed = jnp.concatenate(
            [lax.dynamic_slice_in_dim(grid, spatial_order[place], 1, axis=0) for place in range(tile_count)],
            axis=0,
        )
        placed = jnp.transpose(placed, (1, 0, 2, 3))
        return placed.reshape(seq_count * tile_count * tile_rows, head_width)

    video_queries = arrange(relayed[0])
    video_keys = arrange(relayed[1])
    video_values = arrange(relayed[2])
    keys_text, values_text = (
        lax.all_to_all(text_keys[0], "seq", split_axis=1, concat_axis=0, tiled=True),
        lax.all_to_all(text_values[0], "seq", split_axis=1, concat_axis=0, tiled=True),
    )
    attended_heads = attend(
        video_queries, video_keys, video_values, keys_text, values_text, text_lengths[0]
    )
    attended = lax.all_to_all(attended_heads, "seq", split_axis=0, concat_axis=1, tiled=True)
    return attended[None]


def peer_order(sect_count, tile_count):
    half = tile_count // 2
    steps = sorted(range(tile_count), key=lambda step: abs(step - half))
    pairs = [(o, step) for step in steps for o in reversed(range(sect_count))]
    pairs = [pair for pair in pairs if pair != (0, 0)]
    return pairs


def relay_kernel(
    sizes,
    chunks,
    q_ref, k_ref, v_ref, tk_ref, tv_ref, len_in, place_in,
    out_ref,
    qbuf, kbuf, vbuf, tbuf, obuf, len_ref, place_ref,
    send_sem, recv_sem, text_send, text_recv, out_send, out_recv, scalar_sems, go_sem, pbuf, dbuf,
):
    sect_count, seq_count, tile_count, heads, part_blocks, rows, text_part = sizes
    me_s, me_q, me_d = lax.axis_index("sect"), lax.axis_index("seq"), lax.axis_index("dp")
    mesh_ids = pl.DeviceIdType.MESH
    width = heads * HD
    order = peer_order(sect_count, tile_count)
    block_rows = tile_count * rows
    text_rows = text_part * seq_count
    key_rows = block_rows * seq_count

    def group_peer(offset):
        return lax.rem(me_s + offset[0], sect_count), lax.rem(me_d + offset[1], tile_count)

    barrier = pltpu.get_barrier_semaphore()
    middle = jnp.logical_or(me_d == 1, me_d == 2)
    near = jnp.bitwise_xor(me_d, 3)
    side = jnp.bitwise_xor(me_d, 1)

    def greet(semaphore, flip, step, to_d):
        pl.semaphore_signal(
            semaphore,
            inc=1,
            device_id={
                "sect": jnp.bitwise_xor(me_s, flip),
                "seq": jnp.bitwise_xor(me_q, step),
                "dp": to_d,
            },
            device_id_type=mesh_ids,
        )

    @pl.when(middle)
    def _():
        greet(barrier, 0, 0, near)
        for step in range(seq_count):
            greet(barrier, 0, step, side)
        greet(barrier, 1, 0, side)
        for flip in range(sect_count):
            greet(barrier, flip, 0, jnp.bitwise_xor(me_d, 2))

    @pl.when(jnp.logical_not(middle))
    def _():
        greet(barrier, 1, 0, me_d)
        for flip in range(sect_count):
            greet(barrier, flip, 0, near)
        for step in range(1, seq_count):
            greet(barrier, 0, step, me_d)

    scalars = (
        pltpu.make_async_copy(len_in, len_ref, scalar_sems.at[0]),
        pltpu.make_async_copy(place_in, place_ref, scalar_sems.at[1]),
    )
    for copy in scalars:
        copy.start()

    sources = (q_ref, k_ref, v_ref)
    buffers = (qbuf, kbuf, vbuf)
    texts = (tk_ref, tv_ref)

    def columns_of(chunk):
        return pl.ds(chunk[1] * HD, chunk[2] * HD)

    def pieces(chunk, clip):
        number, cut = chunk[0], chunk[3]
        for at in range(part_blocks if cut else 1):
            some = pl.ds(at, 1) if cut else pl.ds(0, part_blocks)
            there = pl.ds(me_s * part_blocks + at, 1) if cut else pl.ds(me_s * part_blocks, part_blocks)
            arrival = recv_sem.at[chunks.index(chunk), me_s * part_blocks + at if cut else 0]
            yield (
                sources[number].at[clip, some, :, columns_of(chunk)],
                buffers[number].at[there, me_d, :, columns_of(chunk)],
                arrival,
            )

    def send_group(group, flip, turn):
        to_s = jnp.int32(flip - 10) if flip >= 10 else jnp.bitwise_xor(me_s, flip)
        to_d = jnp.bitwise_xor(me_d, turn)
        for chunk in group:
            for source, target, arrival in pieces(chunk, to_s * tile_count + to_d):
                pltpu.make_async_remote_copy(
                    src_ref=source,
                    dst_ref=target,
                    send_sem=send_sem.at[chunk[0]],
                    recv_sem=arrival,
                    device_id={"sect": to_s, "dp": to_d},
                    device_id_type=mesh_ids,
                ).start()

    my_text = pl.ds(me_q * text_part, text_part)

    def copy_own():
        for chunk in chunks:
            for source, target, arrival in pieces(chunk, me_s * tile_count + me_d):
                pltpu.make_async_copy(source, target, arrival).start()
        for number in range(2):
            pltpu.make_async_copy(
                texts[number].at[:, pl.ds(pl.multiple_of(me_q * width, HD), width)],
                tbuf.at[number, my_text],
                text_recv,
            ).start()

    def send_text():
        for step in range(1, seq_count):
            to_q = jnp.bitwise_xor(me_q, step)
            for number in range(2):
                pltpu.make_async_remote_copy(
                    src_ref=texts[number].at[:, pl.ds(pl.multiple_of(to_q * width, HD), width)],
                    dst_ref=tbuf.at[number, my_text],
                    send_sem=text_send,
                    recv_sem=text_recv,
                    device_id={"seq": to_q},
                    device_id_type=mesh_ids,
                ).start()

    def send_all(items):
        for item in items:
            if item == "text":
                send_text()
            elif item == "own":
                copy_own()
            elif item == "go":
                pl.semaphore_wait(go_sem, seq_count)
            else:
                for flip, turn in item[1]:
                    send_group(item[0], flip, turn)

    pl.semaphore_wait(barrier, jnp.where(middle, 1, 1 + sect_count + (seq_count - 1) * 2 + 1 + 1 + sect_count))

    @pl.when(jnp.logical_not(middle))
    def _():
        for step in range(seq_count):
            greet(go_sem, 0, step, side)


    pl.when(me_d == 1)(functools.partial(send_all, MIDS[1]))
    pl.when(me_d == 2)(functools.partial(send_all, MIDS[2]))
    pl.when(jnp.logical_not(middle))(functools.partial(send_all, ENDS))

    factor = math.log2(math.e) / math.sqrt(HD)
    for copy in scalars:
        copy.wait()
    live = lax.broadcasted_iota(jnp.int32, (1, text_rows), 1) < len_ref[0]
    places = [place_ref[slot] for slot in range(tile_count)]
    pltpu.make_async_copy(tbuf, tbuf, text_recv).wait()
    contract_last = (((1,), (1,)), ((), ()))
    waited = set()

    def await_part(number, head, block):
        for index, chunk in enumerate(chunks):
            if chunk[0] != number or not chunk[1] <= head < chunk[1] + chunk[2]:
                continue
            if chunk[3]:
                view = buffers[number].at[block, :, :, columns_of(chunk)]
                pltpu.make_async_copy(view, view, recv_sem.at[index, block]).wait()
            elif index not in waited:
                waited.add(index)
                view = buffers[number].at[:, :, :, columns_of(chunk)]
                pltpu.make_async_copy(view, view, recv_sem.at[index, 0]).wait()

    def in_place(tiles):
        placed = []
        for place in range(tile_count):
            chosen = tiles[0]
            for slot in range(1, tile_count):
                chosen = jnp.where(places[slot] == place, tiles[slot], chosen)
            placed.append(chosen)
        return jnp.concatenate(placed, axis=0)

    def scores_of(queries, keys, keys_text):
        video = lax.dot_general(queries, keys, contract_last, preferred_element_type=jnp.float32)
        text = lax.dot_general(queries, keys_text, contract_last, preferred_element_type=jnp.float32)
        text = jnp.where(live, text, -jnp.inf)
        top = jnp.maximum(jnp.max(video, axis=1, keepdims=True), jnp.max(text, axis=1, keepdims=True))
        video = jnp.exp2((video - top) * factor)
        text = jnp.exp2((text - top) * factor)
        total = jnp.sum(video, axis=1, keepdims=True) + jnp.sum(text, axis=1, keepdims=True)
        return video.astype(jnp.bfloat16), text.astype(jnp.bfloat16), total

    def mix(video, text, total, values, values_text):
        mixed = jnp.dot(video, values, preferred_element_type=jnp.float32)
        mixed += jnp.dot(text, values_text, preferred_element_type=jnp.float32)
        return (mixed / total).astype(jnp.bfloat16)

    def deliver(c, step, block):
        flip = FLIPS[step]
        obuf[c, step] = block
        place = out_ref.at[:, pl.ds(pl.multiple_of((me_q * heads + c) * HD, HD), HD)]
        if flip == 0:
            pltpu.make_async_copy(obuf.at[c, step], place, out_recv).start()
        else:
            pltpu.make_async_remote_copy(
                src_ref=obuf.at[c, step],
                dst_ref=place,
                send_sem=out_send,
                recv_sem=out_recv,
                device_id={"seq": jnp.bitwise_xor(me_q, flip)},
                device_id_type=mesh_ids,
            ).start()

    owners = [jnp.bitwise_xor(me_q, flip) for flip in FLIPS]
    for c in range(heads):
        columns = slice(c * HD, (c + 1) * HD)
        await_part(1, c, None)
        await_part(0, c, None)
        queries = jnp.concatenate(
            [in_place([qbuf[to_q, slot, :, columns] for slot in range(tile_count)]) for to_q in owners],
            axis=0,
        )
        keys = kbuf[:, :, :, columns].reshape(key_rows, HD)
        video, text, total = scores_of(queries, keys, tbuf[0, :, columns])
        if c == heads - 1:
            pbuf[:, :key_rows] = video
            pbuf[:, key_rows:] = text
            dbuf[...] = jnp.broadcast_to(total, dbuf.shape)
        await_part(2, c, None)
        values = vbuf[:, :, :, columns].reshape(key_rows, HD)
        values_text = tbuf[1, :, columns]
        if c < heads - 1:
            mixed = mix(video, text, total, values, values_text)
            for step in range(seq_count):
                deliver(c, step, mixed[step * block_rows : (step + 1) * block_rows])
        else:
            for half in range(HALVES):
                size = key_rows // HALVES
                some = slice(half * size, (half + 1) * size)
                mixed = mix(pbuf[some, :key_rows], pbuf[some, key_rows:], dbuf[some], values, values_text)
                for at in range(size // block_rows):
                    deliver(c, half * (size // block_rows) + at, mixed[at * block_rows : (at + 1) * block_rows])

    for number in range(3):
        view = sources[number].at[pl.ds(0, len(order))]
        pltpu.make_async_copy(view, view, send_sem.at[number]).wait()
    text_view = tbuf.at[:, pl.ds(0, text_part * (seq_count - 1))]
    pltpu.make_async_copy(text_view, text_view, text_send).wait()
    out_view = obuf.at[:, pl.ds(0, seq_count - 1)]
    pltpu.make_async_copy(out_view, out_view, out_send).wait()
    pltpu.make_async_copy(out_ref, out_ref, out_recv).wait()


FLIPS = (2, 3, 1, 0)
HALVES = 4
CHUNKS = [(1, 0, 2, False), (2, 0, 2, False), (0, 0, 2, False), (1, 2, 1, False), (2, 2, 1, False), (0, 2, 1, False), (1, 3, 1, False), (0, 3, 1, False), (2, 3, 1, False)]
ENDS = [([(1, 0, 2, False), (2, 0, 2, False), (0, 0, 2, False)], [(10, 2), (11, 2), (10, 3), (11, 3), (1, 1), (0, 1), (1, 0)]), 'own', 'text', ([(1, 2, 1, False), (2, 2, 1, False), (0, 2, 1, False)], [(10, 2), (11, 2), (10, 3), (11, 3), (1, 1), (0, 1), (1, 0)]), ([(1, 3, 1, False), (0, 3, 1, False)], [(10, 2), (11, 2), (10, 3), (11, 3), (1, 1), (0, 1), (1, 0)]), ([(2, 3, 1, False)], [(10, 2), (11, 2), (10, 3), (11, 3), (1, 1), (0, 1), (1, 0)])]
MIDS = {2: [([(1, 0, 2, False), (2, 0, 2, False), (0, 0, 2, False)], [(0, 3)]), ([(1, 2, 1, False)], [(0, 3)]), 'own', 'go', 'text', ([(1, 0, 2, False), (2, 0, 2, False), (0, 0, 2, False)], [(10, 2), (11, 2), (1, 3)]), ([(1, 0, 2, False), (2, 0, 2, False), (0, 0, 2, False), (1, 2, 1, False), (2, 2, 1, False), (0, 2, 1, False), (1, 3, 1, False), (0, 3, 1, False), (2, 3, 1, False)], [(1, 1), (0, 1), (1, 0)]), ([(1, 2, 1, False), (2, 2, 1, False), (0, 2, 1, False)], [(10, 2)]), ([(1, 3, 1, False), (0, 3, 1, False)], [(10, 2)]), ([(2, 3, 1, False)], [(10, 2)]), ([(1, 2, 1, False), (2, 2, 1, False), (0, 2, 1, False)], [(11, 2)]), ([(1, 3, 1, False), (0, 3, 1, False)], [(11, 2)]), ([(2, 3, 1, False)], [(11, 2)]), ([(1, 2, 1, False)], [(1, 3)]), ([(2, 2, 1, False), (0, 2, 1, False)], [(10, 3), (11, 3)]), ([(1, 3, 1, False), (0, 3, 1, False)], [(10, 3), (11, 3)]), ([(2, 3, 1, False)], [(10, 3), (11, 3)])],
    1: [([(1, 0, 2, False), (2, 0, 2, False), (0, 0, 2, False)], [(0, 3)]), ([(1, 2, 1, False)], [(0, 3)]), 'own', 'go', 'text', ([(1, 0, 2, False), (2, 0, 2, False), (0, 0, 2, False)], [(10, 2), (11, 2), (1, 3)]), ([(1, 0, 2, False), (2, 0, 2, False), (0, 0, 2, False), (1, 2, 1, False), (2, 2, 1, False), (0, 2, 1, False), (1, 3, 1, False), (0, 3, 1, False), (2, 3, 1, False)], [(1, 1), (0, 1), (1, 0)]), ([(1, 2, 1, False), (2, 2, 1, False), (0, 2, 1, False)], [(10, 2)]), ([(1, 3, 1, False), (0, 3, 1, False)], [(10, 2)]), ([(1, 2, 1, False), (2, 2, 1, False), (0, 2, 1, False)], [(11, 2)]), ([(1, 3, 1, False), (0, 3, 1, False)], [(11, 2)]), ([(1, 2, 1, False)], [(1, 3)]), ([(2, 2, 1, False), (0, 2, 1, False)], [(10, 3), (11, 3)]), ([(1, 3, 1, False), (0, 3, 1, False)], [(10, 3), (11, 3)]), ([(2, 3, 1, False)], [(10, 3), (11, 3)]), ([(2, 3, 1, False)], [(10, 2), (11, 2)])]}


def relay_chunks(heads):
    return CHUNKS


def fused_shards(query_tiles, key_tiles, value_tiles, text_keys, text_values, text_lengths, tile_place):
    sect_count, seq_count, tile_count = (lax.axis_size(name) for name in ("sect", "seq", "dp"))
    clips, part_rows, width = query_tiles.shape[1:]
    rows = part_rows * sect_count // seq_count
    heads = width // HD
    part_blocks = part_rows // rows
    text_part, all_width = text_keys.shape[1:]
    out_rows = tile_count * rows
    sizes = (sect_count, seq_count, tile_count, heads, part_blocks, rows, text_part)
    chunks = relay_chunks(heads)
    hbm = pl.BlockSpec(memory_space=pltpu.HBM)
    tiles = pltpu.VMEM((seq_count, tile_count, rows, width), jnp.bfloat16)

    def blocks(piece):
        return piece.reshape(clips, part_blocks, rows, width)

    gathered = pl.pallas_call(
        functools.partial(relay_kernel, sizes, chunks),
        out_shape=pltpu.VMEM((out_rows, all_width), jnp.bfloat16),
        in_specs=[hbm] * 7,
        out_specs=pl.BlockSpec(memory_space=pltpu.VMEM),
        scratch_shapes=[
            tiles,
            tiles,
            tiles,
            pltpu.VMEM((2, text_part * seq_count, width), jnp.bfloat16),
            pltpu.VMEM((heads, seq_count, out_rows, HD), jnp.bfloat16),
            pltpu.SMEM((1,), jnp.int32),
            pltpu.SMEM((tile_count,), jnp.int32),
            pltpu.SemaphoreType.DMA((3,)),
            pltpu.SemaphoreType.DMA((len(chunks), seq_count)),
            pltpu.SemaphoreType.DMA,
            pltpu.SemaphoreType.DMA,
            pltpu.SemaphoreType.DMA,
            pltpu.SemaphoreType.DMA,
            pltpu.SemaphoreType.DMA((2,)),
            pltpu.SemaphoreType.REGULAR,
            pltpu.VMEM((seq_count * out_rows, seq_count * (out_rows + text_part)), jnp.bfloat16),
            pltpu.VMEM((seq_count * out_rows, HD), jnp.float32),
        ],
        compiler_params=pltpu.CompilerParams(
            collective_id=0, has_side_effects=True, vmem_limit_bytes=60 * 2**20
        ),
    )(
        blocks(query_tiles),
        blocks(key_tiles),
        blocks(value_tiles),
        text_keys[0],
        text_values[0],
        text_lengths,
        tile_place,
    )
    return gathered[None]


def solution(mesh):
    in_specs = (
        P("dp", None, "sect", "seq"),
        P("dp", None, "sect", "seq"),
        P("dp", None, "sect", "seq"),
        P(("sect", "dp"), "seq", None),
        P(("sect", "dp"), "seq", None),
        P(("sect", "dp")),
        P(),
    )
    out_specs = P(("sect", "dp"), "seq", None)

    def pick(*operands):
        rows = operands[0].shape[2] * mesh.shape["sect"] // mesh.shape["seq"]
        return (shards if rows % 16 or mesh.shape["seq"] != 4 else fused_shards)(*operands)

    return jax.shard_map(pick, mesh=mesh, in_specs=in_specs, out_specs=out_specs, check_vma=False)
```

```python
import functools
import math

import jax
import jax.numpy as jnp
from jax import lax
from jax.experimental import pallas as pl
from jax.experimental.pallas import tpu as pltpu
from jax.sharding import PartitionSpec as P

HD = 128


def attend(queries_flat, keys_video, values_video, keys_text, values_text, length):
    query_rows, head_width = queries_flat.shape
    head_count = head_width // HD
    score_scale = 1.0 / math.sqrt(HD)
    keys_video = keys_video.reshape(-1, head_count, HD)
    values_video = values_video.reshape(-1, head_count, HD)
    keys_text = keys_text.reshape(-1, head_count, HD)
    values_text = values_text.reshape(-1, head_count, HD)
    live_mask = jnp.arange(keys_text.shape[0], dtype=jnp.int32) < length
    block_rows = math.gcd(query_rows, 512)

    def one_block(query_block):
        score_video = (
            jnp.einsum("qhd,khd->hqk", query_block, keys_video, preferred_element_type=jnp.float32)
            * score_scale
        )
        score_text = (
            jnp.einsum("qhd,khd->hqk", query_block, keys_text, preferred_element_type=jnp.float32)
            * score_scale
        )
        score_text = jnp.where(live_mask[None, None, :], score_text, -jnp.inf)
        row_max = jnp.maximum(jnp.max(score_video, axis=-1), jnp.max(score_text, axis=-1))[
            ..., None
        ]
        expo_video = jnp.exp(score_video - row_max)
        expo_text = jnp.exp(score_text - row_max)
        denominators = jnp.sum(expo_video, axis=-1) + jnp.sum(expo_text, axis=-1)
        mixed = jnp.einsum(
            "hqk,khd->qhd",
            expo_video.astype(jnp.bfloat16),
            values_video,
            preferred_element_type=jnp.float32,
        )
        mixed = mixed + jnp.einsum(
            "hqk,khd->qhd",
            expo_text.astype(jnp.bfloat16),
            values_text,
            preferred_element_type=jnp.float32,
        )
        return (mixed / jnp.transpose(denominators)[:, :, None]).astype(jnp.bfloat16)

    blocks = queries_flat.reshape(query_rows // block_rows, block_rows, head_count, HD)
    return lax.map(one_block, blocks).reshape(query_rows, head_width)


def shards(query_tiles, key_tiles, value_tiles, text_keys, text_values, text_lengths, tile_place):
    tile_count = lax.axis_size("dp")
    sect_count = lax.axis_size("sect")
    part_rows = query_tiles.shape[2]
    head_width = query_tiles.shape[3]
    tile_seq = part_rows * sect_count

    def regroup(piece):
        return piece.reshape(1, sect_count, tile_count, part_rows, head_width)

    relayed = (
        lax.all_to_all(
            lax.all_to_all(regroup(query_tiles), "sect", split_axis=1, concat_axis=3, tiled=True),
            "dp",
            split_axis=2,
            concat_axis=0,
            tiled=True,
        ),
        lax.all_to_all(
            lax.all_to_all(regroup(key_tiles), "sect", split_axis=1, concat_axis=3, tiled=True),
            "dp",
            split_axis=2,
            concat_axis=0,
            tiled=True,
        ),
        lax.all_to_all(
            lax.all_to_all(regroup(value_tiles), "sect", split_axis=1, concat_axis=3, tiled=True),
            "dp",
            split_axis=2,
            concat_axis=0,
            tiled=True,
        ),
    )
    spatial_order = jnp.argsort(tile_place)
    seq_count = lax.axis_size("seq")
    tile_rows = tile_seq // seq_count

    def arrange(piece):
        grid = piece.reshape(tile_count, seq_count, tile_rows, head_width)
        placed = jnp.concatenate(
            [lax.dynamic_slice_in_dim(grid, spatial_order[place], 1, axis=0) for place in range(tile_count)],
            axis=0,
        )
        placed = jnp.transpose(placed, (1, 0, 2, 3))
        return placed.reshape(seq_count * tile_count * tile_rows, head_width)

    video_queries = arrange(relayed[0])
    video_keys = arrange(relayed[1])
    video_values = arrange(relayed[2])
    keys_text, values_text = (
        lax.all_to_all(text_keys[0], "seq", split_axis=1, concat_axis=0, tiled=True),
        lax.all_to_all(text_values[0], "seq", split_axis=1, concat_axis=0, tiled=True),
    )
    attended_heads = attend(
        video_queries, video_keys, video_values, keys_text, values_text, text_lengths[0]
    )
    attended = lax.all_to_all(attended_heads, "seq", split_axis=0, concat_axis=1, tiled=True)
    return attended[None]


def peer_order(sect_count, tile_count):
    half = tile_count // 2
    steps = sorted(range(tile_count), key=lambda step: abs(step - half))
    pairs = [(o, step) for step in steps for o in reversed(range(sect_count))]
    pairs = [pair for pair in pairs if pair != (0, 0)]
    return pairs


def relay_kernel(
    sizes,
    chunks,
    q_ref, k_ref, v_ref, tk_ref, tv_ref, len_in, place_in,
    out_ref,
    qbuf, kbuf, vbuf, tbuf, obuf, len_ref, place_ref,
    send_sem, recv_sem, text_send, text_recv, out_send, out_recv, scalar_sems, go_sem,
):
    sect_count, seq_count, tile_count, heads, part_blocks, rows, text_part = sizes
    me_s, me_q, me_d = lax.axis_index("sect"), lax.axis_index("seq"), lax.axis_index("dp")
    mesh_ids = pl.DeviceIdType.MESH
    width = heads * HD
    order = peer_order(sect_count, tile_count)
    block_rows = tile_count * rows
    text_rows = text_part * seq_count
    key_rows = block_rows * seq_count

    def group_peer(offset):
        return lax.rem(me_s + offset[0], sect_count), lax.rem(me_d + offset[1], tile_count)

    barrier = pltpu.get_barrier_semaphore()
    middle = jnp.logical_or(me_d == 1, me_d == 2)
    near = jnp.bitwise_xor(me_d, 3)
    side = jnp.bitwise_xor(me_d, 1)

    def greet(semaphore, flip, step, to_d):
        pl.semaphore_signal(
            semaphore,
            inc=1,
            device_id={
                "sect": jnp.bitwise_xor(me_s, flip),
                "seq": jnp.bitwise_xor(me_q, step),
                "dp": to_d,
            },
            device_id_type=mesh_ids,
        )

    @pl.when(middle)
    def _():
        greet(barrier, 0, 0, near)
        for step in range(seq_count):
            greet(barrier, 0, step, side)
        greet(barrier, 1, 0, side)
        for flip in range(sect_count):
            greet(barrier, flip, 0, jnp.bitwise_xor(me_d, 2))

    @pl.when(jnp.logical_not(middle))
    def _():
        greet(barrier, 1, 0, me_d)
        for flip in range(sect_count):
            greet(barrier, flip, 0, near)
        for step in range(1, seq_count):
            greet(barrier, 0, step, me_d)

    scalars = (
        pltpu.make_async_copy(len_in, len_ref, scalar_sems.at[0]),
        pltpu.make_async_copy(place_in, place_ref, scalar_sems.at[1]),
    )
    for copy in scalars:
        copy.start()

    sources = (q_ref, k_ref, v_ref)
    buffers = (qbuf, kbuf, vbuf)
    texts = (tk_ref, tv_ref)

    def columns_of(chunk):
        return pl.ds(chunk[1] * HD, chunk[2] * HD)

    def pieces(chunk, clip):
        number, cut = chunk[0], chunk[3]
        for at in [cut - 1 if cut else 0]:
            some = pl.ds(at, 1) if cut else pl.ds(0, part_blocks)
            there = pl.ds(me_s * part_blocks + at, 1) if cut else pl.ds(me_s * part_blocks, part_blocks)
            arrival = recv_sem.at[chunks.index(chunk), me_s * part_blocks + at if cut else 0]
            yield (
                sources[number].at[clip, some, :, columns_of(chunk)],
                buffers[number].at[there, me_d, :, columns_of(chunk)],
                arrival,
            )

    def send_group(group, flip, turn):
        to_s = jnp.bitwise_xor(me_s, flip)
        to_d = jnp.bitwise_xor(me_d, turn)
        for chunk in group:
            for source, target, arrival in pieces(chunk, to_s * tile_count + to_d):
                pltpu.make_async_remote_copy(
                    src_ref=source,
                    dst_ref=target,
                    send_sem=send_sem.at[chunk[0]],
                    recv_sem=arrival,
                    device_id={"sect": to_s, "dp": to_d},
                    device_id_type=mesh_ids,
                ).start()

    my_text = pl.ds(me_q * text_part, text_part)

    def copy_own():
        for chunk in chunks:
            for source, target, arrival in pieces(chunk, me_s * tile_count + me_d):
                pltpu.make_async_copy(source, target, arrival).start()
        for number in range(2):
            pltpu.make_async_copy(
                texts[number].at[:, pl.ds(pl.multiple_of(me_q * width, HD), width)],
                tbuf.at[number, my_text],
                text_recv,
            ).start()

    def send_text():
        for step in range(1, seq_count):
            to_q = jnp.bitwise_xor(me_q, step)
            for number in range(2):
                pltpu.make_async_remote_copy(
                    src_ref=texts[number].at[:, pl.ds(pl.multiple_of(to_q * width, HD), width)],
                    dst_ref=tbuf.at[number, my_text],
                    send_sem=text_send,
                    recv_sem=text_recv,
                    device_id={"seq": to_q},
                    device_id_type=mesh_ids,
                ).start()

    def send_all(items):
        for item in items:
            if item == "text":
                send_text()
            elif item == "own":
                copy_own()
            elif item == "go":
                pl.semaphore_wait(go_sem, seq_count)
            else:
                for flip, turn in item[1]:
                    send_group(item[0], flip, turn)

    pl.semaphore_wait(barrier, jnp.where(middle, 1, 1 + sect_count + (seq_count - 1) * 2 + 1 + 1 + sect_count))

    @pl.when(jnp.logical_not(middle))
    def _():
        for step in range(seq_count):
            greet(go_sem, 0, step, side)


    pl.when(me_d == 1)(functools.partial(send_all, MIDS[1]))
    pl.when(me_d == 2)(functools.partial(send_all, MIDS[2]))
    pl.when(jnp.logical_not(middle))(functools.partial(send_all, ENDS))

    factor = math.log2(math.e) / math.sqrt(HD)
    for copy in scalars:
        copy.wait()
    live = lax.broadcasted_iota(jnp.int32, (1, text_rows), 1) < len_ref[0]
    places = [place_ref[slot] for slot in range(tile_count)]
    pltpu.make_async_copy(tbuf, tbuf, text_recv).wait()
    contract_last = (((1,), (1,)), ((), ()))
    waited = set()

    def await_part(number, head, block, at):
        for index, chunk in enumerate(chunks):
            if chunk[0] != number or not chunk[1] <= head < chunk[1] + chunk[2]:
                continue
            if chunk[3] and chunk[3] != at + 1:
                continue
            if chunk[3]:
                view = buffers[number].at[block, :, :, columns_of(chunk)]
                pltpu.make_async_copy(view, view, recv_sem.at[index, block]).wait()
            elif index not in waited:
                waited.add(index)
                view = buffers[number].at[:, :, :, columns_of(chunk)]
                pltpu.make_async_copy(view, view, recv_sem.at[index, 0]).wait()

    def in_place(tiles):
        placed = []
        for place in range(tile_count):
            chosen = tiles[0]
            for slot in range(1, tile_count):
                chosen = jnp.where(places[slot] == place, tiles[slot], chosen)
            placed.append(chosen)
        return jnp.concatenate(placed, axis=0)

    def attend_rows(queries, keys, values, keys_text, values_text):
        video = lax.dot_general(queries, keys, contract_last, preferred_element_type=jnp.float32)
        text = lax.dot_general(queries, keys_text, contract_last, preferred_element_type=jnp.float32)
        text = jnp.where(live, text, -jnp.inf)
        top = jnp.maximum(jnp.max(video, axis=1, keepdims=True), jnp.max(text, axis=1, keepdims=True))
        video = jnp.exp2((video - top) * factor)
        text = jnp.exp2((text - top) * factor)
        total = jnp.sum(video, axis=1, keepdims=True) + jnp.sum(text, axis=1, keepdims=True)
        mixed = jnp.dot(video.astype(jnp.bfloat16), values, preferred_element_type=jnp.float32)
        mixed += jnp.dot(text.astype(jnp.bfloat16), values_text, preferred_element_type=jnp.float32)
        return (mixed / total).astype(jnp.bfloat16)

    core = lax.rem(me_q, 2)
    row_first = me_q - core
    other_first = jnp.bitwise_xor(row_first, 2)

    def deliver(c, step, block, owner, inner):
        obuf[c, step] = block
        place = out_ref.at[:, pl.ds(pl.multiple_of((me_q * heads + c) * HD, HD), HD)]

        def send():
            pltpu.make_async_remote_copy(
                src_ref=obuf.at[c, step],
                dst_ref=place,
                send_sem=out_send,
                recv_sem=out_recv,
                device_id={"seq": jnp.bitwise_xor(me_q, 1) if inner else owner},
                device_id_type=mesh_ids,
            ).start()

        def keep():
            pltpu.make_async_copy(obuf.at[c, step], place, out_recv).start()

        if inner:
            pl.when(owner == me_q)(keep)
            pl.when(owner != me_q)(send)
        else:
            send()

    whole = [((0, 0), (0, 1), (1, 0), (1, 1))]
    for c in range(heads):
        columns = slice(c * HD, (c + 1) * HD)
        await_part(1, c, None, None)
        await_part(2, c, None, None)
        keys = kbuf[:, :, :, columns].reshape(key_rows, HD)
        values = vbuf[:, :, :, columns].reshape(key_rows, HD)
        for part in whole if c < heads - 1 else LAST:
            owners = [(row_first if inner else other_first) + at for inner, at in part]
            for owner, (inner, at) in zip(owners, part):
                await_part(0, c, owner, at)
            queries = jnp.concatenate(
                [in_place([qbuf[owner, slot, :, columns] for slot in range(tile_count)]) for owner in owners],
                axis=0,
            )
            mixed = attend_rows(queries, keys, values, tbuf[0, :, columns], tbuf[1, :, columns])
            for n, (owner, (inner, at)) in enumerate(zip(owners, part)):
                deliver(c, inner * 2 + at, mixed[n * block_rows : (n + 1) * block_rows], owner, inner)

    for number in range(3):
        view = sources[number].at[pl.ds(0, len(order))]
        pltpu.make_async_copy(view, view, send_sem.at[number]).wait()
    text_view = tbuf.at[:, pl.ds(0, text_part * (seq_count - 1))]
    pltpu.make_async_copy(text_view, text_view, text_send).wait()
    out_view = obuf.at[:, pl.ds(0, seq_count - 1)]
    pltpu.make_async_copy(out_view, out_view, out_send).wait()
    pltpu.make_async_copy(out_ref, out_ref, out_recv).wait()


LAST = [((0, 0), (1, 0)), ((0, 1),), ((1, 1),)]
CHUNKS = [(1, 0, 2, 0), (2, 0, 2, 0), (0, 0, 2, 0), (1, 2, 1, 0), (2, 2, 1, 0), (0, 2, 1, 0), (1, 3, 1, 0), (2, 3, 1, 0), (0, 3, 1, 1), (0, 3, 1, 2)]
ENDS = [([(1, 0, 2, 0), (2, 0, 2, 0), (0, 0, 2, 0)], [(1, 2), (0, 2), (1, 3), (0, 3), (1, 1), (0, 1), (1, 0)]), 'own', 'text', ([(1, 2, 1, 0), (2, 2, 1, 0), (0, 2, 1, 0)], [(1, 2), (0, 2), (1, 3), (0, 3), (1, 1), (0, 1), (1, 0)]), ([(1, 3, 1, 0), (2, 3, 1, 0), (0, 3, 1, 1)], [(1, 2), (0, 2), (1, 3), (0, 3), (1, 1), (0, 1), (1, 0)]), ([(0, 3, 1, 2)], [(1, 2), (0, 2), (1, 3), (0, 3), (1, 1), (0, 1), (1, 0)])]
MIDS = {2: [([(1, 0, 2, 0), (2, 0, 2, 0), (0, 0, 2, 0)], [(0, 3)]), 'own', 'go', 'text', ([(1, 0, 2, 0), (2, 0, 2, 0), (0, 0, 2, 0)], [(1, 2), (0, 2), (1, 3)]), ([(1, 0, 2, 0), (2, 0, 2, 0), (0, 0, 2, 0), (1, 2, 1, 0), (2, 2, 1, 0), (0, 2, 1, 0), (1, 3, 1, 0), (2, 3, 1, 0), (0, 3, 1, 1), (0, 3, 1, 2)], [(1, 1), (0, 1), (1, 0)]), ([(1, 2, 1, 0), (2, 2, 1, 0), (0, 2, 1, 0)], [(1, 2), (0, 2)]), ([(1, 3, 1, 0), (2, 3, 1, 0), (0, 3, 1, 1)], [(1, 2), (0, 2)]), ([(0, 3, 1, 2)], [(1, 2), (0, 2)]), ([(1, 2, 1, 0), (2, 2, 1, 0), (0, 2, 1, 0)], [(1, 3), (0, 3)]), ([(1, 3, 1, 0), (2, 3, 1, 0), (0, 3, 1, 1)], [(1, 3), (0, 3)]), ([(0, 3, 1, 2)], [(1, 3), (0, 3)])],
    1: [([(1, 0, 2, 0), (2, 0, 2, 0), (0, 0, 2, 0)], [(0, 3)]), 'own', 'go', 'text', ([(1, 0, 2, 0), (2, 0, 2, 0), (0, 0, 2, 0)], [(1, 2), (0, 2), (1, 3)]), ([(1, 0, 2, 0), (2, 0, 2, 0), (0, 0, 2, 0), (1, 2, 1, 0), (2, 2, 1, 0), (0, 2, 1, 0), (1, 3, 1, 0), (2, 3, 1, 0), (0, 3, 1, 1), (0, 3, 1, 2)], [(1, 1), (0, 1), (1, 0)]), ([(1, 2, 1, 0), (2, 2, 1, 0), (0, 2, 1, 0)], [(1, 2), (0, 2)]), ([(1, 3, 1, 0), (2, 3, 1, 0), (0, 3, 1, 1)], [(1, 2), (0, 2)]), ([(1, 2, 1, 0), (2, 2, 1, 0), (0, 2, 1, 0)], [(1, 3), (0, 3)]), ([(1, 3, 1, 0), (2, 3, 1, 0), (0, 3, 1, 1)], [(1, 3), (0, 3)]), ([(0, 3, 1, 2)], [(1, 3), (0, 3)]), ([(0, 3, 1, 2)], [(1, 2), (0, 2)])]}


def relay_chunks(heads):
    return CHUNKS


def fused_shards(query_tiles, key_tiles, value_tiles, text_keys, text_values, text_lengths, tile_place):
    sect_count, seq_count, tile_count = (lax.axis_size(name) for name in ("sect", "seq", "dp"))
    clips, part_rows, width = query_tiles.shape[1:]
    rows = part_rows * sect_count // seq_count
    heads = width // HD
    part_blocks = part_rows // rows
    text_part, all_width = text_keys.shape[1:]
    out_rows = tile_count * rows
    sizes = (sect_count, seq_count, tile_count, heads, part_blocks, rows, text_part)
    chunks = relay_chunks(heads)
    hbm = pl.BlockSpec(memory_space=pltpu.HBM)
    tiles = pltpu.VMEM((seq_count, tile_count, rows, width), jnp.bfloat16)

    def blocks(piece):
        return piece.reshape(clips, part_blocks, rows, width)

    gathered = pl.pallas_call(
        functools.partial(relay_kernel, sizes, chunks),
        out_shape=pltpu.VMEM((out_rows, all_width), jnp.bfloat16),
        in_specs=[hbm] * 7,
        out_specs=pl.BlockSpec(memory_space=pltpu.VMEM),
        scratch_shapes=[
            tiles,
            tiles,
            tiles,
            pltpu.VMEM((2, text_part * seq_count, width), jnp.bfloat16),
            pltpu.VMEM((heads, seq_count, out_rows, HD), jnp.bfloat16),
            pltpu.SMEM((1,), jnp.int32),
            pltpu.SMEM((tile_count,), jnp.int32),
            pltpu.SemaphoreType.DMA((3,)),
            pltpu.SemaphoreType.DMA((len(chunks), seq_count)),
            pltpu.SemaphoreType.DMA,
            pltpu.SemaphoreType.DMA,
            pltpu.SemaphoreType.DMA,
            pltpu.SemaphoreType.DMA,
            pltpu.SemaphoreType.DMA((2,)),
            pltpu.SemaphoreType.REGULAR,
        ],
        compiler_params=pltpu.CompilerParams(
            collective_id=0, has_side_effects=True, vmem_limit_bytes=60 * 2**20
        ),
    )(
        blocks(query_tiles),
        blocks(key_tiles),
        blocks(value_tiles),
        text_keys[0],
        text_values[0],
        text_lengths,
        tile_place,
    )
    return gathered[None]


def solution(mesh):
    in_specs = (
        P("dp", None, "sect", "seq"),
        P("dp", None, "sect", "seq"),
        P("dp", None, "sect", "seq"),
        P(("sect", "dp"), "seq", None),
        P(("sect", "dp"), "seq", None),
        P(("sect", "dp")),
        P(),
    )
    out_specs = P(("sect", "dp"), "seq", None)

    def pick(*operands):
        rows = operands[0].shape[2] * mesh.shape["sect"] // mesh.shape["seq"]
        return (shards if rows % 16 or mesh.shape["seq"] != 4 else fused_shards)(*operands)

    return jax.shard_map(pick, mesh=mesh, in_specs=in_specs, out_specs=out_specs, check_vma=0)
```
